256 devices in a mesh: ctx: 16 (over y, x), head: 16 (over z, core).
Axes of the slice: x: 4, y: 4, z: 8, core: 2. Of those that a mesh axis runs over, the one named last changes fastest.
Arguments:
- queries: bfloat16 [2, 4096, 8192], P(None, 'ctx', 'head'), may hold values from -4.5 to 4.5
- key_rows: bfloat16 [2, 4096, 512], P(None, 'ctx'), may hold values from -4.5 to 4.5
- value_rows: bfloat16 [2, 4096, 512], P(None, 'ctx'), may hold values from -6 to 6
- out_weight: bfloat16 [8192, 8192], P('head'), may hold values from -0.0625 to 0.0625
- span_owner: int32 [2, 16], replicated, may hold values from 0 to 15, each once within a row
- vertical_blocks: int32 [64, 4], replicated, may hold values from 0 to 63, as said below
- slash_offsets: int32 [64, 4], replicated, may hold values from 1 to 63, as said below
Outputs:
- projected: bfloat16 [2, 4096, 8192], P(None, ('ctx', 'head'))
The draws below stay inside these ranges and needn't reach their ends.
Inputs may be any that keep to these rules, and one draw needn't show every extreme that they name: `vertical_blocks`: the 4 entries of a head are distinct block numbers. `slash_offsets`: the 4 entries of a head are distinct.
All inputs are finite; a program needn't handle non-finite values.
Results may differ from the reference program's by a relative error of at most 0.017.
Values may be sent and summed in bfloat16 or wider, within the bound.
No kernel may reach another device: no remote copies, remote signals or barrier semaphores. Data moves between devices by JAX's collectives and lax.ppermute only.
A program may use at most 64 MiB of HBM per device.

```python
import math
import jax
import jax.numpy as jnp
from jax import lax

DW = 8192
QH = 64
KVH = 4
HD = 128
BLK = 128
SPAN = 256
STEPS = 2
NV = 4
NS = 4
SPANS = 16
ROWS = 4096
HEAD_GROUPS = 16
NB = 64


def draw_queries(key, part):
    full_shape = (STEPS, ROWS, QH * HD)
    entries = jnp.clip(jax.random.normal(jax.random.fold_in(key, 11), full_shape, jnp.float32), -4.5, 4.5)
    return entries.astype(jnp.bfloat16)


def draw_key_rows(key, part):
    full_shape = (STEPS, ROWS, KVH * HD)
    entries = jnp.clip(jax.random.normal(jax.random.fold_in(key, 12), full_shape, jnp.float32), -4.5, 4.5)
    return entries.astype(jnp.bfloat16)


def distinct_rows(key, lowest, highest, pick_count, row_total):

    def one_row(row_index):
        shuffled = lowest + jax.random.permutation(jax.random.fold_in(key, row_index), highest - lowest)
        return shuffled[:pick_count].astype(jnp.int32)
    shuffled_rows = jax.vmap(one_row)(jnp.arange(row_total))
    middle = lowest + 1 + jax.random.permutation(jax.random.fold_in(key, row_total + 7), highest - lowest - 2)
    first_row = jnp.concatenate([jnp.array([lowest, highest - 1], dtype=jnp.int32), middle[:pick_count - 2].astype(jnp.int32)])
    return shuffled_rows.at[0].set(first_row)


def draw_vertical_blocks(key, part):
    return distinct_rows(jax.random.fold_in(key, 21), 0, NB, NV, QH)


def draw_slash_offsets(key, part):
    return distinct_rows(jax.random.fold_in(key, 22), 1, NB, NS, QH)


def steps_of(own_key, shape, cuts, low, high):
    loudness = 1.0
    for position, parts in cuts:
        draws = jax.random.uniform(jax.random.fold_in(jax.random.fold_in(own_key, 6), position), (parts,), jnp.float32, low / len(cuts), high / len(cuts))
        loudness = loudness * jnp.repeat(jnp.exp(draws), shape[position] // parts).reshape((-1,) + (1,) * (len(shape) - 1 - position))
    return loudness


def gaussian(key, shape, scale, most, shards=(), kind=jnp.bfloat16):
    values = jax.random.normal(key, shape, jnp.float32) * scale
    if len(shards) > 0:
        values = steps_of(key, shape, shards, -0.22, 0.18) * values
    return jnp.clip(values, min=-most, max=most).astype(kind)


def setup_inputs(seed: int = 0) -> dict:
    seeds = jax.random.split(jax.random.key(seed), 8)
    queries = draw_queries(jax.random.fold_in(seeds[7], 71), 0)
    key_rows = draw_key_rows(jax.random.fold_in(seeds[7], 71), 0)
    value_rows = gaussian(seeds[2], (STEPS, ROWS, KVH * HD), 1.0, 6.0, ((1, 16),))
    out_weight = gaussian(seeds[3], (QH * HD, DW), (QH * HD) ** -0.5, 0.0625, ((0, 16),))
    span_owner = jax.vmap(lambda own: jax.random.permutation(own, SPANS))(jax.random.split(seeds[4], STEPS)).reshape((STEPS, SPANS)).astype(jnp.int32)
    vertical_blocks = draw_vertical_blocks(jax.random.fold_in(seeds[7], 71), 0)
    slash_offsets = draw_slash_offsets(jax.random.fold_in(seeds[7], 71), 0)
    return {"queries": queries, "key_rows": key_rows, "value_rows": value_rows, "out_weight": out_weight, "span_owner": span_owner, "vertical_blocks": vertical_blocks, "slash_offsets": slash_offsets}


def tile_blocks(block_ids, vertical, slanted, owner_flat, span_blocks, span_count):
    column = block_ids[:, None]
    vert_rows = jnp.broadcast_to(vertical[None, :], (block_ids.shape[0], vertical.shape[0]))
    slash_rows = column - slanted[None, :]
    vert_valid = vert_rows < column
    repeated = jnp.any(slash_rows[:, :, None] == vertical[None, None, :], axis=2)
    slash_valid = (slash_rows >= 0) & jnp.logical_not(repeated)
    chosen = jnp.concatenate([column, vert_rows, slash_rows], axis=1)
    allowed = jnp.concatenate([jnp.ones_like(column, dtype=bool), vert_valid, slash_valid], axis=1)
    chosen = jnp.where(allowed, chosen, column)
    span_index = chosen // span_blocks
    slot_ids = jnp.arange(owner_flat.shape[0], dtype=jnp.int32)
    holder = lax.optimization_barrier(jnp.sum(jnp.where(span_index[:, :, None] == slot_ids[None, None, :], owner_flat[None, None, :], 0), axis=2))
    step_index = span_index // span_count
    stored = (step_index * span_count + holder) * span_blocks + chosen % span_blocks
    return (stored.astype(jnp.int32), allowed)

def block_mask(allowed, block_rows):
    positions = jnp.arange(block_rows, dtype=jnp.int32)
    causal = positions[None, :] <= positions[:, None]
    tile_count = allowed.shape[1]
    first_tile = jnp.arange(tile_count, dtype=jnp.int32) == 0
    inside = causal[None, :, None, :] | jnp.logical_not(first_tile)[None, None, :, None]
    visible = allowed[:, None, :, None] & inside
    return visible.reshape(allowed.shape[0], block_rows, tile_count * block_rows)

def attend_head(query_tile_set, key_store, value_store, stored, allowed):
    block_count = stored.shape[0]
    tile_count = stored.shape[1]
    block_rows = query_tile_set.shape[1]
    head_features = query_tile_set.shape[2]
    key_tile_set = jnp.take(key_store, stored.reshape(-1), axis=0).reshape(block_count, tile_count * block_rows, head_features)
    value_tile_set = jnp.take(value_store, stored.reshape(-1), axis=0).reshape(block_count, tile_count * block_rows, head_features)
    logit_scores = jnp.einsum('zcs,zvs->zcv', query_tile_set.astype(jnp.float32), key_tile_set.astype(jnp.float32)) * (1.0 / math.sqrt(head_features))
    logit_scores = jnp.where(block_mask(allowed, block_rows), logit_scores, -jnp.inf)
    largest = lax.optimization_barrier(jnp.max(logit_scores, axis=2, keepdims=True))
    weights = jnp.exp(logit_scores - largest)
    totals = lax.optimization_barrier(jnp.sum(weights, axis=2, keepdims=True))
    rounded_values = lax.optimization_barrier(weights.astype(jnp.bfloat16))
    mixed_output = jnp.einsum('ynj,yjw->ynw', rounded_values.astype(jnp.float32), value_tile_set.astype(jnp.float32))
    return (mixed_output / totals).astype(jnp.bfloat16)

def reference(queries, key_rows, value_rows, out_weight, span_owner, vertical_blocks, slash_offsets):
    span_blocks = SPAN // BLK
    owners = span_owner.astype(jnp.int32)
    owner_flat = owners.reshape(-1)
    device_ids = jnp.arange(SPANS, dtype=jnp.int32)
    places = lax.optimization_barrier(jnp.sum(device_ids[None, None, :] * (owners[:, None, :] == device_ids[None, :, None]).astype(jnp.int32), axis=2)).astype(jnp.int32)
    step_ids = jnp.arange(STEPS, dtype=jnp.int32)[:, None, None]
    inner_ids = jnp.arange(span_blocks, dtype=jnp.int32)[None, None, :]
    block_ids = ((step_ids * SPANS + places[:, :, None]) * span_blocks + inner_ids).reshape(-1).astype(jnp.int32)
    group_size = QH // KVH

    def one_head(head_index):
        kv_head = head_index // group_size
        query_tile_set = lax.dynamic_slice_in_dim(queries, head_index * HD, HD, 2).reshape(-1, BLK, HD)
        key_store = lax.dynamic_slice_in_dim(key_rows, kv_head * HD, HD, 2).reshape(-1, BLK, HD)
        value_store = lax.dynamic_slice_in_dim(value_rows, kv_head * HD, HD, 2).reshape(-1, BLK, HD)
        vertical = lax.dynamic_index_in_dim(vertical_blocks, head_index, 0, keepdims=False).astype(jnp.int32)
        slanted = lax.dynamic_index_in_dim(slash_offsets, head_index, 0, keepdims=False).astype(jnp.int32)
        stored, allowed = tile_blocks(block_ids, vertical, slanted, owner_flat, span_blocks, SPANS)
        return attend_head(query_tile_set, key_store, value_store, stored, allowed).reshape(STEPS, ROWS, HD)
    heads_out = lax.map(one_head, jnp.arange(QH, dtype=jnp.int32))
    attended = jnp.transpose(heads_out, (1, 2, 0, 3)).reshape(STEPS * ROWS, QH * HD)
    group_width = QH * HD // HEAD_GROUPS

    def add_group(running, group_index):
        columns = lax.dynamic_slice_in_dim(attended, group_index * group_width, group_width, 1)
        weight_rows = lax.dynamic_slice_in_dim(out_weight, group_index * group_width, group_width, 0)
        partial_sum = jnp.dot(columns, weight_rows, preferred_element_type=jnp.float32)
        rounded_values = lax.optimization_barrier(partial_sum.astype(jnp.bfloat16))
        return (running + rounded_values.astype(jnp.float32), None)
    running = lax.scan(add_group, jnp.zeros((STEPS * ROWS, DW), jnp.float32), jnp.arange(HEAD_GROUPS, dtype=jnp.int32))[0]
    return running.astype(jnp.bfloat16).reshape(STEPS, ROWS, DW)
```

```python
import functools
import math

import jax
import jax.numpy as jnp
from jax import lax
from jax.experimental import pallas as pl
from jax.experimental.pallas import tpu as pltpu
from jax.sharding import PartitionSpec as P

QH = 64
KVH = 4
HD = 128
BLK = 128
STEPS = 2
SPANS = 16
LOCAL_HEADS = 4
SPAN = 256
NV = 4
NS = 4
DW = 8192
TILE = 512
HIDDEN = -1e30


def core_swap(heads):
    return [(h, h ^ 1) for h in range(heads)]


def shift_z(heads, amount):
    chips = heads // 2
    return [(h, ((h // 2 + amount) % chips) * 2 + h % 2) for h in range(heads)]


def step_kernel(step, *refs):
    stores = 2 * (step + 1)
    owner, vertical, slash, q_hbm, w_hbm = refs[:5]
    kv_hbm = refs[5 : 5 + stores]
    send_hbm, own_hbm = refs[5 + stores : 7 + stores]
    q_v, kv_v, w_v, att_v, out_v, sem_in, sem_kv, sem_out = refs[7 + stores :]
    device = lax.axis_index("ctx")
    head_group = lax.axis_index("head")
    core = lax.rem(head_group, 2)

    copies = [pltpu.make_async_copy(q_hbm.at[step], q_v, sem_in.at[0])]
    for index in range(step + 1):
        for side in range(2):
            half = core if side == 0 else 1 - core
            copies.append(
                pltpu.make_async_copy(
                    kv_hbm[2 * index + side], kv_v.at[index, half], sem_kv.at[index, side]
                )
            )
    w_copy = pltpu.make_async_copy(w_hbm, w_v, sem_in.at[1])
    for copy in copies:
        copy.start()
    w_copy.start()

    place = jnp.int32(0)
    for p in range(SPANS):
        place += jnp.where(owner[step, p] == device, p, 0)
    for copy in copies:
        copy.wait()

    rows_at = lax.broadcasted_iota(jnp.int32, (BLK, BLK), 0)
    cols_at = lax.broadcasted_iota(jnp.int32, (BLK, BLK), 1)
    causal = cols_at <= rows_at

    def tile(block, part):
        span = block // 2
        which = span // SPANS
        holder = owner[which, lax.rem(span, SPANS)]
        if step == 0:
            which = 0
        return kv_v[which, lax.rem(block, 2), holder, part]

    def one_pair(pair, carry):
        local_head = pair // 2
        inner = lax.rem(pair, 2)
        head = head_group * LOCAL_HEADS + local_head
        block = (step * SPANS + place) * 2 + inner
        q_rows = pl.ds(pl.multiple_of(inner * BLK, BLK), BLK)
        q_cols = pl.ds(pl.multiple_of(local_head * HD, HD), HD)
        q = q_v[q_rows, q_cols]
        picked = [vertical[head, n] for n in range(NV)]
        blocks = [block]
        shown = [None]
        for k in picked:
            good = k < block
            blocks.append(jnp.where(good, k, block))
            shown.append(good)
        for n in range(NS):
            k = block - slash[head, n]
            good = k >= 0
            for other in picked:
                good = good & (k != other)
            blocks.append(jnp.where(good, k, block))
            shown.append(good)
        scores = []
        for k, good in zip(blocks, shown):
            s = lax.dot_general(
                q, tile(k, 0), (((1,), (1,)), ((), ())), preferred_element_type=jnp.float32
            )
            if good is None:
                s = jnp.where(causal, s, HIDDEN)
            else:
                s = jnp.where(good, s, HIDDEN)
            scores.append(s)
        largest = functools.reduce(jnp.maximum, scores)
        largest = jnp.max(largest, axis=1, keepdims=True)
        scale = 1.0 / math.sqrt(HD)
        weights = [jnp.exp((s - largest) * scale) for s in scores]
        totals = jnp.sum(functools.reduce(jnp.add, weights), axis=1, keepdims=True)
        mixed = None
        for k, w in zip(blocks, weights):
            part = jnp.dot(w.astype(jnp.bfloat16), tile(k, 1), preferred_element_type=jnp.float32)
            mixed = part if mixed is None else mixed + part
        result = (mixed / totals).astype(jnp.bfloat16)
        for group in range(BLK // 16):
            z = inner * 4 + group // 2
            start = jnp.where(core == group % 2, 128, 0) + z * 16
            att_v[pl.ds(pl.multiple_of(start, 16), 16), q_cols] = result[group * 16 : group * 16 + 16]
        return carry

    lax.fori_loop(0, LOCAL_HEADS * 2, one_pair, 0)

    w_copy.wait()
    attended = att_v[...]

    def out_copies(n):
        cols = pl.ds(pl.multiple_of(n * TILE, TILE), TILE)
        return (
            pltpu.make_async_copy(out_v.at[pl.ds(0, 128), cols], send_hbm.at[:, cols], sem_out.at[n, 0]),
            pltpu.make_async_copy(out_v.at[pl.ds(128, 128), cols], own_hbm.at[:, cols], sem_out.at[n, 1]),
        )

    def project(n, carry):
        cols = pl.ds(pl.multiple_of(n * TILE, TILE), TILE)
        out_v[:, cols] = jnp.dot(
            attended, w_v[:, cols], preferred_element_type=jnp.float32
        ).astype(jnp.bfloat16)
        for copy in out_copies(n):
            copy.start()
        return carry

    lax.fori_loop(0, DW // TILE, project, 0)

    def finish(n, carry):
        for copy in out_copies(n):
            copy.wait()
        return carry

    lax.fori_loop(0, DW // TILE, finish, 0)


def run_step(step, owner, vertical, slash, queries, weight, stores):
    anywhere = pl.BlockSpec(memory_space=pl.ANY)
    scalars = pl.BlockSpec(memory_space=pltpu.SMEM)
    half = jax.ShapeDtypeStruct((SPAN // 2, DW), jnp.bfloat16)
    return pl.pallas_call(
        functools.partial(step_kernel, step),
        out_shape=(half, half),
        in_specs=[scalars] * 3 + [anywhere] * (2 + len(stores)),
        out_specs=(anywhere, anywhere),
        scratch_shapes=[
            pltpu.VMEM((SPAN, LOCAL_HEADS * HD), jnp.bfloat16),
            pltpu.VMEM((step + 1, 2, SPANS, 2, BLK, HD), jnp.bfloat16),
            pltpu.VMEM((LOCAL_HEADS * HD, DW), jnp.bfloat16),
            pltpu.VMEM((SPAN, LOCAL_HEADS * HD), jnp.bfloat16),
            pltpu.VMEM((SPAN, DW), jnp.bfloat16),
            pltpu.SemaphoreType.DMA((2,)),
            pltpu.SemaphoreType.DMA((step + 1, 2)),
            pltpu.SemaphoreType.DMA((DW // TILE, 2)),
        ],
        cost_estimate=pl.CostEstimate(
            flops=2 * SPAN * LOCAL_HEADS * HD * DW, bytes_accessed=20 << 20, transcendentals=0
        ),
        name=f"attend_project_{step}",
    )(owner, vertical, slash, queries, weight, *stores)


def local(queries, key_rows, value_rows, out_weight, span_owner, vertical_blocks, slash_offsets):
    heads = lax.axis_size("head")
    chips = heads // 2
    head_group = lax.axis_index("head")
    core = lax.rem(head_group, 2)
    z = head_group // 2
    kv_head = head_group * LOCAL_HEADS // (QH // KVH)
    swap = core_swap(heads)

    def own_block(rows, step):
        return lax.dynamic_slice(rows[step], (core * BLK, kv_head * HD), (BLK, HD))

    stores = []
    tie = None
    partials = []
    for step in range(STEPS):
        mine = jnp.stack([own_block(key_rows, step), own_block(value_rows, step)])
        if tie is not None:
            mine = mine + tie
        gathered = lax.all_to_all(
            jnp.broadcast_to(mine[None], (SPANS, 2, BLK, HD)), "ctx", 0, 0, tiled=True
        )
        tie = gathered[0, 0, 0, 0] * 0
        stores += [gathered, lax.ppermute(gathered, "head", swap)]
        partials.append(
            run_step(step, span_owner, vertical_blocks, slash_offsets, queries, out_weight, list(stores))
        )

    outputs = []
    for step in range(STEPS):
        send, own = partials[step]
        other = lax.ppermute(send, "head", swap).reshape(chips, 16, DW)
        own = own.reshape(chips, 16, DW)

        def chunk(offset):
            index = lax.rem(z + offset + chips, chips)
            return lax.dynamic_index_in_dim(own, index, 0, False).astype(
                jnp.float32
            ) + lax.dynamic_index_in_dim(other, index, 0, False).astype(jnp.float32)

        arrived = []
        for direction in (1, -1):
            far = chips // 2 if (direction == 1) == (step == 0) else chips // 2 - 1
            moving = None
            for distance in range(far, 0, -1):
                total = chunk(direction * distance)
                if moving is not None:
                    total = total + moving.astype(jnp.float32)
                moving = lax.ppermute(total.astype(jnp.bfloat16), "head", shift_z(heads, direction))
            arrived.append(moving)
        total = chunk(0) + arrived[0].astype(jnp.float32) + arrived[1].astype(jnp.float32)
        outputs.append(total.astype(jnp.bfloat16))
    return jnp.stack(outputs)


def solution(mesh):
    in_specs = (
        P(None, "ctx", "head"),
        P(None, "ctx", None),
        P(None, "ctx", None),
        P("head", None),
        P(),
        P(),
        P(),
    )
    out_specs = P(None, ("ctx", "head"), None)
    return jax.shard_map(local, mesh=mesh, in_specs=in_specs, out_specs=out_specs, check_vma=False)
```

```python
import functools
import math

import jax
import jax.numpy as jnp
from jax import lax
from jax.experimental import pallas as pl
from jax.experimental.pallas import tpu as pltpu
from jax.sharding import PartitionSpec as P


QH = 64
KVH = 4
HD = 128
BLK = 128
STEPS = 2
SPANS = 16
LOCAL_HEADS = 4
SPAN = 256
NV = 4
NS = 4
DW = 8192
TILE = 512
HALVES = 2
WIDTH = DW // HALVES
TILES = 1 + NV + NS
PAIRS = LOCAL_HEADS * 2
HIDDEN = -1e30
MIB = 1 << 20


ANYWHERE = pl.BlockSpec(memory_space=pl.ANY)
SCALARS = pl.BlockSpec(memory_space=pltpu.SMEM)
IN_HBM = pl.BlockSpec(memory_space=pltpu.HBM)
IN_VMEM = pl.BlockSpec(memory_space=pltpu.VMEM)


def core_swap(heads):
    return [(h, h ^ 1) for h in range(heads)]


def shift_z(heads, amount):
    chips = heads // 2
    return [(h, ((h // 2 + amount) % chips) * 2 + h % 2) for h in range(heads)]


def after(x, *earlier):
    return pl.pallas_call(
        lambda *refs: None,
        out_shape=jax.ShapeDtypeStruct(x.shape, x.dtype),
        in_specs=[ANYWHERE] * (1 + len(earlier)),
        out_specs=ANYWHERE,
        input_output_aliases={0: 0},
        compiler_params=pltpu.CompilerParams(vmem_limit_bytes=MIB),
        name="after",
    )(x, *earlier)


def plan_kernel(owner, vertical, slash, table):
    device = lax.axis_index("ctx")
    head_group = lax.axis_index("head")

    def one_pair(index, carry):
        step = index // PAIRS
        pair = lax.rem(index, PAIRS)
        head = head_group * LOCAL_HEADS + pair // 2

        def look(p, place):
            return place + jnp.where(owner[step, p] == device, p, 0)

        place = lax.fori_loop(0, SPANS, look, jnp.int32(0))
        block = (step * SPANS + place) * 2 + lax.rem(pair, 2)

        def put(slot, k, good):
            k = jnp.where(good, k, block)
            span = k // 2
            which = span // SPANS
            holder = owner[which, lax.rem(span, SPANS)]
            stored = (which * 2 + lax.rem(k, 2)) * SPANS + holder
            table[index * TILES + slot] = stored * 2 + jnp.where(good, 1, 0)

        put(0, block, block >= 0)
        picked = [vertical[head, n] for n in range(NV)]
        for n, k in enumerate(picked):
            put(1 + n, k, k < block)
        for n in range(NS):
            k = block - slash[head, n]
            good = k >= 0
            for other in picked:
                good = good & (k != other)
            put(1 + NV + n, k, good)
        return carry

    lax.fori_loop(0, STEPS * PAIRS, one_pair, 0)


def make_plan(owner, vertical, slash):
    return pl.pallas_call(
        plan_kernel,
        out_shape=jax.ShapeDtypeStruct((STEPS * PAIRS * TILES,), jnp.int32),
        in_specs=[SCALARS] * 3,
        out_specs=SCALARS,
        compiler_params=pltpu.CompilerParams(vmem_limit_bytes=MIB),
        name="plan",
    )(owner, vertical, slash)


def attend_kernel(step, *refs):
    stores = 2 * (step + 1)
    table, q_hbm, w_hbm = refs[:3]
    kv_hbm = refs[3 : 3 + stores]
    out, send, own, q_v, kv_v, w_v, sems = refs[-7:]
    core = lax.rem(lax.axis_index("head"), 2)

    copies = [pltpu.make_async_copy(q_hbm.at[step], q_v, sems.at[0])]
    for index in range(step + 1):
        for side in range(2):
            half = core if side == 0 else 1 - core
            start = pl.multiple_of((2 * index + half) * SPANS, SPANS)
            copies.append(
                pltpu.make_async_copy(
                    kv_hbm[2 * index + side],
                    kv_v.at[pl.ds(start, SPANS)],
                    sems.at[1 + 2 * index + side],
                )
            )
    w_copy = pltpu.make_async_copy(w_hbm.at[:, pl.ds(0, WIDTH)], w_v, sems.at[1 + stores])
    for copy in copies:
        copy.start()
    w_copy.start()
    for copy in copies:
        copy.wait()

    rows_at = lax.broadcasted_iota(jnp.int32, (BLK, BLK), 0)
    cols_at = lax.broadcasted_iota(jnp.int32, (BLK, BLK), 1)
    causal = cols_at <= rows_at
    scale = 1.0 / math.sqrt(HD)

    def one_pair(local_head, inner):
        q_cols = pl.ds(pl.multiple_of(local_head * HD, HD), HD)
        q = q_v[inner * BLK : (inner + 1) * BLK, q_cols]
        first = ((step * PAIRS) + local_head * 2 + inner) * TILES
        codes = [table[first + n] for n in range(TILES)]
        places = [lax.shift_right_logical(code, 1) for code in codes]
        keys = jnp.concatenate([kv_v[place, 0] for place in places], axis=0)
        all_scores = lax.dot_general(
            q, keys, (((1,), (1,)), ((), ())), preferred_element_type=jnp.float32
        )
        scores = []
        for n in range(TILES):
            s = all_scores[:, n * BLK : (n + 1) * BLK]
            good = causal if n == 0 else (codes[n] & 1) == 1
            scores.append(jnp.where(good, s, HIDDEN))
        largest = functools.reduce(jnp.maximum, scores)
        largest = jnp.max(largest, axis=1, keepdims=True)
        weights = [jnp.exp((s - largest) * scale) for s in scores]
        totals = jnp.sum(functools.reduce(jnp.add, weights), axis=1, keepdims=True)
        values = jnp.concatenate([kv_v[place, 1] for place in places], axis=0)
        mixed = jnp.dot(
            jnp.concatenate([w.astype(jnp.bfloat16) for w in weights], axis=1),
            values,
            preferred_element_type=jnp.float32,
        )
        result = (mixed / totals).astype(jnp.bfloat16)
        for group in range(BLK // 16):
            z = inner * 4 + group // 2
            start = jnp.where(core == group % 2, 128, 0) + z * 16
            out[pl.ds(pl.multiple_of(start, 16), 16), q_cols] = result[group * 16 : group * 16 + 16]

    def one_head(local_head, carry):
        for inner in range(2):
            one_pair(local_head, inner)
        return carry

    lax.fori_loop(0, LOCAL_HEADS, one_head, 0)
    w_copy.wait()
    project_tiles(out[...], w_v, send, own, lambda n: None)


def attend(step, table, queries, weight, stores, earlier):
    shape = jax.ShapeDtypeStruct((SPAN // 2, WIDTH), jnp.bfloat16)
    return pl.pallas_call(
        functools.partial(attend_kernel, step),
        out_shape=(jax.ShapeDtypeStruct((SPAN, LOCAL_HEADS * HD), jnp.bfloat16), shape, shape),
        in_specs=[SCALARS] + [IN_HBM] * 2 + [ANYWHERE] * (len(stores) + len(earlier)),
        out_specs=(IN_VMEM, IN_VMEM, IN_VMEM),
        scratch_shapes=[
            pltpu.VMEM((SPAN, LOCAL_HEADS * HD), jnp.bfloat16),
            pltpu.VMEM(((step + 1) * 2 * SPANS, 2, BLK, HD), jnp.bfloat16),
            pltpu.VMEM((LOCAL_HEADS * HD, WIDTH), jnp.bfloat16),
            pltpu.SemaphoreType.DMA((2 + 2 * (step + 1),)),
        ],
        cost_estimate=pl.CostEstimate(
            flops=4 * PAIRS * TILES * BLK * BLK * HD, bytes_accessed=8 * MIB, transcendentals=0
        ),
        compiler_params=pltpu.CompilerParams(vmem_limit_bytes=16 * MIB),
    )(table, queries, weight, *stores, *earlier)


def project_tiles(left, weight, send, own, ready):
    def one_tile(n, carry):
        cols = pl.ds(pl.multiple_of(n * TILE, TILE), TILE)
        ready(n)
        result = jnp.dot(left, weight[:, cols], preferred_element_type=jnp.float32)
        result = result.astype(jnp.bfloat16)
        send[:, cols] = result[: SPAN // 2]
        own[:, cols] = result[SPAN // 2 :]
        return carry

    lax.fori_loop(0, WIDTH // TILE, one_tile, 0)


def project_kernel(half, attended, w_hbm, send, own, w_v, sems):
    def copy_of(n):
        cols = pl.ds(pl.multiple_of(n * TILE, TILE), TILE)
        w_cols = pl.ds(pl.multiple_of(half * WIDTH + n * TILE, TILE), TILE)
        return pltpu.make_async_copy(w_hbm.at[:, w_cols], w_v.at[:, cols], sems.at[n])

    for n in range(WIDTH // TILE):
        copy_of(n).start()
    project_tiles(attended[...], w_v, send, own, lambda n: copy_of(n).wait())


def project(half, attended, weight):
    depth = LOCAL_HEADS * HD
    shape = jax.ShapeDtypeStruct((SPAN // 2, WIDTH), jnp.bfloat16)
    return pl.pallas_call(
        functools.partial(project_kernel, half),
        out_shape=(shape, shape),
        in_specs=[IN_VMEM, IN_HBM],
        out_specs=(IN_VMEM, IN_VMEM),
        scratch_shapes=[
            pltpu.VMEM((depth, WIDTH), jnp.bfloat16),
            pltpu.SemaphoreType.DMA((WIDTH // TILE,)),
        ],
        cost_estimate=pl.CostEstimate(
            flops=2 * SPAN * depth * WIDTH, bytes_accessed=6 * MIB, transcendentals=0
        ),
        compiler_params=pltpu.CompilerParams(vmem_limit_bytes=10 * MIB),
    )(attended, weight)


def local(queries, key_rows, value_rows, out_weight, span_owner, vertical_blocks, slash_offsets):
    heads = lax.axis_size("head")
    chips = heads // 2
    head_group = lax.axis_index("head")
    core = lax.rem(head_group, 2)
    z = head_group // 2
    kv_head = head_group * LOCAL_HEADS // (QH // KVH)
    swap = core_swap(heads)

    table = make_plan(span_owner, vertical_blocks, slash_offsets)

    def own_block(rows, step):
        return lax.dynamic_slice(rows, (step, core * BLK, kv_head * HD), (1, BLK, HD))

    gathered = []
    for step in range(STEPS):
        mine = jnp.concatenate([own_block(key_rows, step), own_block(value_rows, step)])
        mine = jnp.broadcast_to(mine[None], (SPANS, 2, BLK, HD))
        if gathered:
            mine = after(mine, gathered[0])
        gathered.append(lax.all_to_all(mine, "ctx", 0, 0, tiled=True))

    def chunk(stream, offset):
        index = lax.rem(z + offset + chips, chips)
        own, other = stream
        return lax.dynamic_index_in_dim(own, index, 0, False).astype(
            jnp.float32
        ) + lax.dynamic_index_in_dim(other, index, 0, False).astype(jnp.float32)

    moving = {}
    sent = {}

    def hop(step, half, distance):
        for direction in (1, -1):
            far = chips // 2 if (direction == 1) == (half == 0) else chips // 2 - 1
            if distance > far:
                continue
            key = (step, half, direction)
            total = chunk(streams[step, half], direction * distance)
            if key in moving:
                total = total + moving[key].astype(jnp.float32)
            total = total.astype(jnp.bfloat16)
            sent[key] = total
            moving[key] = lax.ppermute(total, "head", shift_z(heads, direction))

    def sent_by(step):
        return [value for key, value in sent.items() if key[0] == step]

    stores = []
    streams = {}
    far = chips // 2

    def compute(step, earlier):
        mine = gathered[step]
        stores.extend([mine, lax.ppermute(mine, "head", swap)])
        attended, send, own = attend(step, table, queries, out_weight, stores, earlier)
        for half in range(HALVES):
            if half > 0:
                send, own = project(half, attended, out_weight)
            other = lax.ppermute(send, "head", swap)
            streams[step, half] = (
                own.reshape(chips, 16, WIDTH),
                other.reshape(chips, 16, WIDTH),
            )

    def hops(step, distance):
        for half in range(HALVES):
            hop(step, half, distance)

    compute(0, [])
    hops(0, far)
    hops(0, far - 1)
    gathered[1] = after(gathered[1], *sent_by(0))
    compute(1, [])
    hops(1, far)
    hops(0, far - 2)
    hops(0, far - 3)
    for distance in range(far - 1, 0, -1):
        hops(1, distance)

    outputs = []
    for step in range(STEPS):
        columns = []
        for half in range(HALVES):
            total = chunk(streams[step, half], 0)
            for direction in (1, -1):
                total = total + moving[step, half, direction].astype(jnp.float32)
            columns.append(total.astype(jnp.bfloat16))
        outputs.append(jnp.concatenate(columns, axis=1)[None])
    return jnp.concatenate(outputs)


def solution(mesh):
    in_specs = (
        P(None, "ctx", "head"),
        P(None, "ctx", None),
        P(None, "ctx", None),
        P("head", None),
        P(),
        P(),
        P(),
    )
    out_specs = P(None, ("ctx", "head"), None)


    return jax.shard_map(
        local, mesh=mesh, in_specs=in_specs, out_specs=out_specs, check_vma=False
    )
```

```python
import functools
import math

import jax
import jax.numpy as jnp
from jax import lax
from jax.experimental import pallas as pl
from jax.experimental.pallas import tpu as pltpu
from jax.sharding import PartitionSpec as P


QH = 64
KVH = 4
HD = 128
BLK = 128
STEPS = 2
SPANS = 16
LOCAL_HEADS = 4
SPAN = 256
NV = 4
NS = 4
DW = 8192
TILE = 512
HALVES = 2
WIDTH = DW // HALVES
TILES = 1 + NV + NS
PAIRS = LOCAL_HEADS * 2
HIDDEN = -1e30
MIB = 1 << 20
GRANT = 56 * MIB


ANYWHERE = pl.BlockSpec(memory_space=pl.ANY)
SCALARS = pl.BlockSpec(memory_space=pltpu.SMEM)
IN_HBM = pl.BlockSpec(memory_space=pltpu.HBM)
IN_VMEM = pl.BlockSpec(memory_space=pltpu.VMEM)


def core_swap(heads):
    return [(h, h ^ 1) for h in range(heads)]


def shift_z(heads, amount):
    chips = heads // 2
    return [(h, ((h // 2 + amount) % chips) * 2 + h % 2) for h in range(heads)]


def plan_kernel(owner, vertical, slash, table):
    device = lax.axis_index("ctx")
    head_group = lax.axis_index("head")

    def one_pair(index, carry):
        step = index // PAIRS
        pair = lax.rem(index, PAIRS)
        head = head_group * LOCAL_HEADS + pair // 2

        def look(p, place):
            return place + jnp.where(owner[step, p] == device, p, 0)

        place = lax.fori_loop(0, SPANS, look, jnp.int32(0))
        block = (step * SPANS + place) * 2 + lax.rem(pair, 2)

        def put(slot, k, good):
            k = jnp.where(good, k, block)
            span = k // 2
            which = span // SPANS
            holder = owner[which, lax.rem(span, SPANS)]
            stored = (which * 2 + lax.rem(k, 2)) * SPANS + holder
            table[index * TILES + slot] = stored * 2 + jnp.where(good, 1, 0)

        put(0, block, block >= 0)
        picked = [vertical[head, n] for n in range(NV)]
        for n, k in enumerate(picked):
            put(1 + n, k, k < block)
        for n in range(NS):
            k = block - slash[head, n]
            good = k >= 0
            for other in picked:
                good = good & (k != other)
            put(1 + NV + n, k, good)
        return carry

    lax.fori_loop(0, STEPS * PAIRS, one_pair, 0)


def make_plan(owner, vertical, slash):
    return pl.pallas_call(
        plan_kernel,
        out_shape=jax.ShapeDtypeStruct((STEPS * PAIRS * TILES,), jnp.int32),
        in_specs=[SCALARS] * 3,
        out_specs=SCALARS,
        compiler_params=pltpu.CompilerParams(vmem_limit_bytes=MIB),
        name="plan",
    )(owner, vertical, slash)


def attend_kernel(step, *refs):
    stores = 2 * (step + 1)
    table, q_hbm, w_hbm = refs[:3]
    kv_hbm = refs[3 : 3 + stores]
    out, send, own, q_v, kv_v, w_v, sems = refs[-7:]
    core = lax.rem(lax.axis_index("head"), 2)

    copies = [pltpu.make_async_copy(q_hbm.at[step], q_v, sems.at[0])]
    for index in range(step + 1):
        for side in range(2):
            half = core if side == 0 else 1 - core
            start = pl.multiple_of((2 * index + half) * SPANS, SPANS)
            copies.append(
                pltpu.make_async_copy(
                    kv_hbm[2 * index + side],
                    kv_v.at[pl.ds(start, SPANS)],
                    sems.at[1 + 2 * index + side],
                )
            )
    w_copy = pltpu.make_async_copy(w_hbm.at[:, pl.ds(0, WIDTH)], w_v, sems.at[1 + stores])
    for copy in copies:
        copy.start()
    w_copy.start()
    for copy in copies:
        copy.wait()

    rows_at = lax.broadcasted_iota(jnp.int32, (BLK, BLK), 0)
    cols_at = lax.broadcasted_iota(jnp.int32, (BLK, BLK), 1)
    causal = cols_at <= rows_at
    scale = 1.0 / math.sqrt(HD)

    def one_pair(local_head, inner):
        q_cols = pl.ds(pl.multiple_of(local_head * HD, HD), HD)
        q = q_v[inner * BLK : (inner + 1) * BLK, q_cols]
        first = ((step * PAIRS) + local_head * 2 + inner) * TILES
        codes = [table[first + n] for n in range(TILES)]
        places = [lax.shift_right_logical(code, 1) for code in codes]
        keys = jnp.concatenate([kv_v[place, 0] for place in places], axis=0)
        all_scores = lax.dot_general(
            q, keys, (((1,), (1,)), ((), ())), preferred_element_type=jnp.float32
        )
        scores = []
        for n in range(TILES):
            s = all_scores[:, n * BLK : (n + 1) * BLK]
            good = causal if n == 0 else (codes[n] & 1) == 1
            scores.append(jnp.where(good, s, HIDDEN))
        largest = functools.reduce(jnp.maximum, scores)
        largest = jnp.max(largest, axis=1, keepdims=True)
        weights = [jnp.exp((s - largest) * scale) for s in scores]
        totals = jnp.sum(functools.reduce(jnp.add, weights), axis=1, keepdims=True)
        values = jnp.concatenate([kv_v[place, 1] for place in places], axis=0)
        mixed = jnp.dot(
            jnp.concatenate([w.astype(jnp.bfloat16) for w in weights], axis=1),
            values,
            preferred_element_type=jnp.float32,
        )
        result = (mixed / totals).astype(jnp.bfloat16)
        for group in range(BLK // 16):
            z = inner * 4 + group // 2
            start = jnp.where(core == group % 2, 128, 0) + z * 16
            out[pl.ds(pl.multiple_of(start, 16), 16), q_cols] = result[group * 16 : group * 16 + 16]

    def one_head(local_head, carry):
        for inner in range(2):
            one_pair(local_head, inner)
        return carry

    lax.fori_loop(0, LOCAL_HEADS, one_head, 0)
    w_copy.wait()
    project_tiles(out[...], w_v, send, own, lambda n: None)


def attend(step, table, queries, weight, stores, earlier):
    shape = jax.ShapeDtypeStruct((SPAN // 2, WIDTH), jnp.bfloat16)
    return pl.pallas_call(
        functools.partial(attend_kernel, step),
        out_shape=(jax.ShapeDtypeStruct((SPAN, LOCAL_HEADS * HD), jnp.bfloat16), shape, shape),
        in_specs=[SCALARS] + [IN_HBM] * 2 + [ANYWHERE] * (len(stores) + len(earlier)),
        out_specs=(IN_VMEM, IN_VMEM, IN_VMEM),
        scratch_shapes=[
            pltpu.VMEM((SPAN, LOCAL_HEADS * HD), jnp.bfloat16),
            pltpu.VMEM(((step + 1) * 2 * SPANS, 2, BLK, HD), jnp.bfloat16),
            pltpu.VMEM((LOCAL_HEADS * HD, WIDTH), jnp.bfloat16),
            pltpu.SemaphoreType.DMA((2 + 2 * (step + 1),)),
        ],
        cost_estimate=pl.CostEstimate(
            flops=4 * PAIRS * TILES * BLK * BLK * HD, bytes_accessed=8 * MIB, transcendentals=0
        ),
        compiler_params=pltpu.CompilerParams(vmem_limit_bytes=GRANT),
    )(table, queries, weight, *stores, *earlier)


def project_tiles(left, weight, send, own, ready):
    def one_tile(n, carry):
        cols = pl.ds(pl.multiple_of(n * TILE, TILE), TILE)
        ready(n)
        result = jnp.dot(left, weight[:, cols], preferred_element_type=jnp.float32)
        result = result.astype(jnp.bfloat16)
        send[:, cols] = result[: SPAN // 2]
        own[:, cols] = result[SPAN // 2 :]
        return carry

    lax.fori_loop(0, WIDTH // TILE, one_tile, 0)


def project_kernel(half, attended, w_hbm, send, own, w_v, sems):
    def copy_of(n):
        cols = pl.ds(pl.multiple_of(n * TILE, TILE), TILE)
        w_cols = pl.ds(pl.multiple_of(half * WIDTH + n * TILE, TILE), TILE)
        return pltpu.make_async_copy(w_hbm.at[:, w_cols], w_v.at[:, cols], sems.at[n])

    for n in range(WIDTH // TILE):
        copy_of(n).start()
    project_tiles(attended[...], w_v, send, own, lambda n: copy_of(n).wait())


def project(half, attended, weight):
    depth = LOCAL_HEADS * HD
    shape = jax.ShapeDtypeStruct((SPAN // 2, WIDTH), jnp.bfloat16)
    return pl.pallas_call(
        functools.partial(project_kernel, half),
        out_shape=(shape, shape),
        in_specs=[IN_VMEM, IN_HBM],
        out_specs=(IN_VMEM, IN_VMEM),
        scratch_shapes=[
            pltpu.VMEM((depth, WIDTH), jnp.bfloat16),
            pltpu.SemaphoreType.DMA((WIDTH // TILE,)),
        ],
        cost_estimate=pl.CostEstimate(
            flops=2 * SPAN * depth * WIDTH, bytes_accessed=6 * MIB, transcendentals=0
        ),
        compiler_params=pltpu.CompilerParams(vmem_limit_bytes=GRANT),
    )(attended, weight)


def pair_sums(own, other, chips):
    def kernel(own_ref, other_ref, *outs):
        z = lax.axis_index("head") // 2
        for offset in range(chips):
            index = lax.rem(z + offset, chips)
            total = own_ref[index].astype(jnp.float32) + other_ref[index].astype(jnp.float32)
            outs[offset][...] = total.astype(jnp.bfloat16)

    rows = own.shape[0] // chips
    shape = (chips, rows, own.shape[1])
    return pl.pallas_call(
        kernel,
        out_shape=[jax.ShapeDtypeStruct(shape[1:], own.dtype)] * chips,
        in_specs=[IN_VMEM] * 2,
        out_specs=[IN_VMEM] * chips,
        cost_estimate=pl.CostEstimate(flops=0, bytes_accessed=3 * MIB, transcendentals=0),
        compiler_params=pltpu.CompilerParams(vmem_limit_bytes=8 * MIB),
    )(own.reshape(shape), other.reshape(shape))


def local(queries, key_rows, value_rows, out_weight, span_owner, vertical_blocks, slash_offsets):
    heads = lax.axis_size("head")
    chips = heads // 2
    head_group = lax.axis_index("head")
    core = lax.rem(head_group, 2)
    kv_head = head_group * LOCAL_HEADS // (QH // KVH)
    swap = core_swap(heads)

    table = make_plan(span_owner, vertical_blocks, slash_offsets)

    def own_block(rows, step):
        return lax.dynamic_slice(rows, (step, core * BLK, kv_head * HD), (1, BLK, HD))

    gathered = []
    for step in range(STEPS):
        mine = jnp.concatenate([own_block(key_rows, step), own_block(value_rows, step)])
        mine = jnp.broadcast_to(mine[None], (SPANS, 2, BLK, HD))
        gathered.append(lax.all_to_all(mine, "ctx", 0, 0, tiled=True))

    moving = {}

    def hop(step, half, distance):
        for direction in (1, -1):
            far = chips // 2 if (direction == 1) == (half == 0) else chips // 2 - 1
            if distance > far:
                continue
            key = (step, half, direction)
            total = streams[step, half][(direction * distance) % chips]
            if key in moving:
                total = total.astype(jnp.float32) + moving[key].astype(jnp.float32)
            total = total.astype(jnp.bfloat16)
            moving[key] = lax.ppermute(total, "head", shift_z(heads, direction))

    stores = []
    streams = {}
    far = chips // 2

    def compute(step, earlier):
        mine = gathered[step]
        stores.extend([mine, lax.ppermute(mine, "head", swap)])
        attended, send, own = attend(step, table, queries, out_weight, stores, earlier)
        for half in range(HALVES):
            if half > 0:
                send, own = project(half, attended, out_weight)
            other = lax.ppermute(send, "head", swap)
            streams[step, half] = pair_sums(own, other, chips)

    def hops(step, distance):
        for half in range(HALVES):
            hop(step, half, distance)

    compute(0, [])
    hops(0, far)
    hops(0, far - 1)
    compute(1, [])
    hops(1, far)
    hops(0, far - 2)
    hops(0, far - 3)
    for distance in range(far - 1, 0, -1):
        hops(1, distance)

    outputs = []
    for step in range(STEPS):
        columns = []
        for half in range(HALVES):
            total = streams[step, half][0].astype(jnp.float32)
            for direction in (1, -1):
                total = total + moving[step, half, direction].astype(jnp.float32)
            columns.append(total.astype(jnp.bfloat16))
        outputs.append(jnp.concatenate(columns, axis=1)[None])
    return jnp.concatenate(outputs)


def solution(mesh):
    in_specs = (
        P(None, "ctx", "head"),
        P(None, "ctx", None),
        P(None, "ctx", None),
        P("head", None),
        P(),
        P(),
        P(),
    )
    out_specs = P(None, ("ctx", "head"), None)


    return jax.shard_map(local, mesh=mesh, in_specs=in_specs, out_specs=out_specs, check_vma=False)
```

```python
import functools
import math

import jax
import jax.numpy as jnp
from jax import lax
from jax.experimental import pallas as pl
from jax.experimental.pallas import tpu as pltpu
from jax.sharding import PartitionSpec as P


QH = 64
KVH = 4
HD = 128
BLK = 128
STEPS = 2
SPANS = 16
LOCAL_HEADS = 4
SPAN = 256
NV = 4
NS = 4
DW = 8192
TILE = 512
HALVES = 2
WIDTH = DW // HALVES
TILES = 1 + NV + NS
PAIRS = LOCAL_HEADS * 2
ROWS = STEPS * SPAN
HIDDEN = -1e30
MIB = 1 << 20
GRANT = 56 * MIB


ANYWHERE = pl.BlockSpec(memory_space=pl.ANY)
SCALARS = pl.BlockSpec(memory_space=pltpu.SMEM)
IN_HBM = pl.BlockSpec(memory_space=pltpu.HBM)
IN_VMEM = pl.BlockSpec(memory_space=pltpu.VMEM)


def core_swap(heads):
    return [(h, h ^ 1) for h in range(heads)]


def shift_z(heads, amount):
    chips = heads // 2
    return [(h, ((h // 2 + amount) % chips) * 2 + h % 2) for h in range(heads)]


def plan_kernel(owner, vertical, slash, table):
    device = lax.axis_index("ctx")
    head_group = lax.axis_index("head")

    def one_pair(index, carry):
        step = index // PAIRS
        pair = lax.rem(index, PAIRS)
        head = head_group * LOCAL_HEADS + pair // 2

        def look(p, place):
            return place + jnp.where(owner[step, p] == device, p, 0)

        place = lax.fori_loop(0, SPANS, look, jnp.int32(0))
        block = (step * SPANS + place) * 2 + lax.rem(pair, 2)

        def put(slot, k, good):
            k = jnp.where(good, k, block)
            span = k // 2
            which = span // SPANS
            holder = owner[which, lax.rem(span, SPANS)]
            stored = (which * 2 + lax.rem(k, 2)) * SPANS + holder
            table[index * TILES + slot] = stored * 2 + jnp.where(good, 1, 0)

        put(0, block, block >= 0)
        picked = [vertical[head, n] for n in range(NV)]
        for n, k in enumerate(picked):
            put(1 + n, k, k < block)
        for n in range(NS):
            k = block - slash[head, n]
            good = k >= 0
            for other in picked:
                good = good & (k != other)
            put(1 + NV + n, k, good)
        return carry

    lax.fori_loop(0, STEPS * PAIRS, one_pair, 0)


def make_plan(owner, vertical, slash):
    return pl.pallas_call(
        plan_kernel,
        out_shape=jax.ShapeDtypeStruct((STEPS * PAIRS * TILES,), jnp.int32),
        in_specs=[SCALARS] * 3,
        out_specs=SCALARS,
        compiler_params=pltpu.CompilerParams(vmem_limit_bytes=MIB),
        name="plan",
    )(owner, vertical, slash)


def attend_kernel(table, q_hbm, mine, other, out, q_v, kv_v, s_0, s_1, m_0, m_1, p_0, p_1, sems):
    core = lax.rem(lax.axis_index("head"), 2)

    copies = [pltpu.make_async_copy(q_hbm, q_v, sems.at[0])]
    for step in range(STEPS):
        for side, store in enumerate((mine, other)):
            half = core if side == 0 else 1 - core
            start = pl.multiple_of((2 * step + half) * SPANS, SPANS)
            copies.append(
                pltpu.make_async_copy(
                    store.at[:, step], kv_v.at[pl.ds(start, SPANS)], sems.at[1 + 2 * step + side]
                )
            )
    for copy in copies:
        copy.start()
    for copy in copies[:3]:
        copy.wait()

    rows_at = lax.broadcasted_iota(jnp.int32, (BLK, BLK), 0)
    cols_at = lax.broadcasted_iota(jnp.int32, (BLK, BLK), 1)
    causal = cols_at <= rows_at
    factor = math.log2(math.e) / math.sqrt(HD)

    def parts(pair):
        step = pair // PAIRS
        head = lax.rem(pair // 2, LOCAL_HEADS)
        return step, pl.ds(pl.multiple_of(head * HD, HD), HD)

    def score(pair, inner, s_v, m_v):
        step, cols = parts(pair)
        q = q_v[step, inner * BLK : (inner + 1) * BLK, cols]
        codes = [table[pair * TILES + n] for n in range(TILES)]
        keys = jnp.concatenate(
            [kv_v[lax.shift_right_logical(code, 1), 0] for code in codes], axis=0
        )
        found = lax.dot_general(
            q, keys, (((1,), (1,)), ((), ())), preferred_element_type=jnp.float32
        )
        largest = None
        for n in range(TILES):
            s = found[:, n * BLK : (n + 1) * BLK]
            s = jnp.where(causal if n == 0 else (codes[n] & 1) == 1, s, HIDDEN)
            s_v[:, n * BLK : (n + 1) * BLK] = s
            largest = s if largest is None else jnp.maximum(largest, s)
        m_v[...] = largest

    def finish(pair, inner, s_v, m_v, p_v):
        step, cols = parts(pair)
        chunk = 32
        totals = []
        for row in range(0, BLK, chunk):
            rows = slice(row, row + chunk)
            shift = jnp.max(m_v[rows], axis=1, keepdims=True) * factor
            total = None
            for n in range(TILES):
                at = slice(n * BLK, (n + 1) * BLK)
                w = jnp.exp2(s_v[rows, at] * factor - shift)
                p_v[rows, at] = w.astype(jnp.bfloat16)
                total = w if total is None else total + w
            totals.append(jnp.sum(total, axis=1, keepdims=True))
        values = jnp.concatenate(
            [kv_v[lax.shift_right_logical(table[pair * TILES + n], 1), 1] for n in range(TILES)],
            axis=0,
        )
        mixed = jnp.dot(p_v[...], values, preferred_element_type=jnp.float32)
        result = (mixed / jnp.concatenate(totals, axis=0)).astype(jnp.bfloat16)
        for group in range(BLK // 16):
            z = inner * 4 + group // 2
            start = jnp.where(core == group % 2, ROWS // 2, 0) + step * (SPAN // 2) + z * 16
            out[pl.ds(pl.multiple_of(start, 16), 16), cols] = result[group * 16 : group * 16 + 16]

    last = STEPS * PAIRS - 2
    score(0, 0, s_0, m_0)

    def two_pairs(index, carry):
        pair = index * 2

        @pl.when(index == PAIRS // 2 - 1)
        def _():
            for copy in copies[3:]:
                copy.wait()

        score(pair + 1, 1, s_1, m_1)
        finish(pair, 0, s_0, m_0, p_0)
        score(jnp.minimum(pair + 2, last), 0, s_0, m_0)
        finish(pair + 1, 1, s_1, m_1, p_1)
        return carry

    lax.fori_loop(0, STEPS * PAIRS // 2, two_pairs, 0)


def attend(table, queries, mine, other):
    keys = TILES * BLK
    return pl.pallas_call(
        attend_kernel,
        out_shape=jax.ShapeDtypeStruct((ROWS, LOCAL_HEADS * HD), jnp.bfloat16),
        in_specs=[SCALARS] + [ANYWHERE] * 3,
        out_specs=IN_VMEM,
        scratch_shapes=[
            pltpu.VMEM((STEPS, SPAN, LOCAL_HEADS * HD), jnp.bfloat16),
            pltpu.VMEM((STEPS * 2 * SPANS, 2, BLK, HD), jnp.bfloat16),
            pltpu.VMEM((BLK, keys), jnp.float32),
            pltpu.VMEM((BLK, keys), jnp.float32),
            pltpu.VMEM((BLK, BLK), jnp.float32),
            pltpu.VMEM((BLK, BLK), jnp.float32),
            pltpu.VMEM((BLK, keys), jnp.bfloat16),
            pltpu.VMEM((BLK, keys), jnp.bfloat16),
            pltpu.SemaphoreType.DMA((1 + 2 * STEPS,)),
        ],
        cost_estimate=pl.CostEstimate(
            flops=8 * PAIRS * TILES * BLK * BLK * HD, bytes_accessed=8 * MIB, transcendentals=0
        ),
        compiler_params=pltpu.CompilerParams(vmem_limit_bytes=12 * MIB),
        name="attend",
    )(table, queries, mine, other)


def project_kernel(half, attended, w_hbm, send, own, w_v, out_v, in_sems, out_sems):
    tiles = WIDTH // TILE

    def columns(n):
        return pl.ds(pl.multiple_of(n * TILE, TILE), TILE)

    def copy_in(n):
        source = pl.ds(pl.multiple_of(half * WIDTH + n * TILE, TILE), TILE)
        return pltpu.make_async_copy(w_hbm.at[:, source], w_v.at[:, columns(n)], in_sems.at[n])

    def copies_out(n):
        return [
            pltpu.make_async_copy(
                out_v.at[pl.ds(side * (ROWS // 2), ROWS // 2), columns(n)],
                target.at[:, columns(n)],
                out_sems.at[n, side],
            )
            for side, target in enumerate((send, own))
        ]

    for n in range(tiles):
        copy_in(n).start()

    def one_tile(n, carry):
        copy_in(n).wait()
        for rows in (slice(0, ROWS // 2), slice(ROWS // 2, ROWS)):
            out_v[rows, columns(n)] = jnp.dot(
                attended[rows], w_v[:, columns(n)], preferred_element_type=jnp.float32
            ).astype(jnp.bfloat16)
        for copy in copies_out(n):
            copy.start()
        return carry

    lax.fori_loop(0, tiles, one_tile, 0)

    def end(n, carry):
        for copy in copies_out(n):
            copy.wait()
        return carry

    lax.fori_loop(0, tiles, end, 0)


def project(half, attended, weight):
    depth = LOCAL_HEADS * HD
    shape = jax.ShapeDtypeStruct((ROWS // 2, WIDTH), jnp.bfloat16)
    return pl.pallas_call(
        functools.partial(project_kernel, half),
        out_shape=(shape, shape),
        in_specs=[IN_VMEM, IN_HBM],
        out_specs=(ANYWHERE, ANYWHERE),
        scratch_shapes=[
            pltpu.VMEM((depth, WIDTH), jnp.bfloat16),
            pltpu.VMEM((ROWS, WIDTH), jnp.bfloat16),
            pltpu.SemaphoreType.DMA((WIDTH // TILE,)),
            pltpu.SemaphoreType.DMA((WIDTH // TILE, 2)),
        ],
        cost_estimate=pl.CostEstimate(
            flops=2 * ROWS * depth * WIDTH, bytes_accessed=8 * MIB, transcendentals=0
        ),
        compiler_params=pltpu.CompilerParams(vmem_limit_bytes=GRANT),
    )(attended, weight)


def pair_sums(own, other, chips):
    def kernel(own_ref, other_ref, *outs):
        z = lax.axis_index("head") // 2
        for step in range(STEPS):
            for offset in range(chips):
                index = step * chips + lax.rem(z + offset, chips)
                total = own_ref[index].astype(jnp.float32) + other_ref[index].astype(jnp.float32)
                outs[step * chips + offset][...] = total.astype(jnp.bfloat16)

    shape = (STEPS * chips, own.shape[0] // (STEPS * chips), own.shape[1])
    sums = pl.pallas_call(
        kernel,
        out_shape=[jax.ShapeDtypeStruct(shape[1:], own.dtype)] * (STEPS * chips),
        in_specs=[IN_VMEM] * 2,
        out_specs=[IN_VMEM] * (STEPS * chips),
        cost_estimate=pl.CostEstimate(flops=0, bytes_accessed=6 * MIB, transcendentals=0),
        compiler_params=pltpu.CompilerParams(vmem_limit_bytes=8 * MIB),
    )(own.reshape(shape), other.reshape(shape))
    return [sums[step * chips : (step + 1) * chips] for step in range(STEPS)]


def local(queries, key_rows, value_rows, out_weight, span_owner, vertical_blocks, slash_offsets):
    heads = lax.axis_size("head")
    chips = heads // 2
    head_group = lax.axis_index("head")
    core = lax.rem(head_group, 2)
    kv_head = head_group * LOCAL_HEADS // (QH // KVH)
    swap = core_swap(heads)

    table = make_plan(span_owner, vertical_blocks, slash_offsets)

    def own_block(rows):
        return lax.dynamic_slice(rows, (0, core * BLK, kv_head * HD), (STEPS, BLK, HD))

    block = jnp.stack([own_block(key_rows), own_block(value_rows)], axis=1)
    block = jnp.broadcast_to(block[None], (SPANS, STEPS, 2, BLK, HD))
    mine = lax.all_to_all(block, "ctx", 0, 0, tiled=True)
    other = lax.ppermute(mine, "head", swap)
    attended = attend(table, queries, mine, other)

    streams = {}
    for half in range(HALVES):
        send, own = project(half, attended, out_weight)
        got = lax.ppermute(send, "head", swap)
        for step, sums in enumerate(pair_sums(own, got, chips)):
            streams[step, half] = sums

    moving = {}
    far = chips // 2

    def hop(step, half, direction, number):
        longest = far if (direction == 1) == (half == 0) else far - 1
        distance = longest - number
        if distance < 1:
            return
        key = (step, half, direction)
        total = streams[step, half][(direction * distance) % chips]
        if key in moving:
            total = total.astype(jnp.float32) + moving[key].astype(jnp.float32)
        total = total.astype(jnp.bfloat16)
        moving[key] = lax.ppermute(total, "head", shift_z(heads, direction))

    for number in range(far):
        for side in (1, -1):
            for half in range(HALVES):
                for step in range(STEPS):
                    hop(step, half, side, number)

    outputs = []
    for step in range(STEPS):
        columns = []
        for half in range(HALVES):
            total = streams[step, half][0].astype(jnp.float32)
            for direction in (1, -1):
                total = total + moving[step, half, direction].astype(jnp.float32)
            columns.append(total.astype(jnp.bfloat16))
        outputs.append(jnp.concatenate(columns, axis=1)[None])
    return jnp.concatenate(outputs)


def solution(mesh):
    in_specs = (
        P(None, "ctx", "head"),
        P(None, "ctx", None),
        P(None, "ctx", None),
        P("head", None),
        P(),
        P(),
        P(),
    )
    out_specs = P(None, ("ctx", "head"), None)

    return jax.shard_map(local, mesh=mesh, in_specs=in_specs, out_specs=out_specs, check_vma=False)
```

```python
import functools
import math

import jax
import jax.numpy as jnp
from jax import lax
from jax.experimental import pallas as pl
from jax.experimental.pallas import tpu as pltpu
from jax.sharding import PartitionSpec as P


QH = 64
KVH = 4
HD = 128
BLK = 128
STEPS = 2
SPANS = 16
LOCAL_HEADS = 4
SPAN = 256
NV = 4
NS = 4
DW = 8192
TILE = 512
HALVES = 2
WIDTH = DW // HALVES
TILES = 1 + NV + NS
PAIRS = LOCAL_HEADS * 2
HIDDEN = -1e30
MIB = 1 << 20
GRANT = 24 * MIB


ANYWHERE = pl.BlockSpec(memory_space=pl.ANY)
SCALARS = pl.BlockSpec(memory_space=pltpu.SMEM)
IN_HBM = pl.BlockSpec(memory_space=pltpu.HBM)
IN_VMEM = pl.BlockSpec(memory_space=pltpu.VMEM)


def core_swap(heads):
    return [(h, h ^ 1) for h in range(heads)]


def shift_z(heads, amount):
    chips = heads // 2
    return [(h, ((h // 2 + amount) % chips) * 2 + h % 2) for h in range(heads)]


def plan_kernel(owner, vertical, slash, table):
    device = lax.axis_index("ctx")
    head_group = lax.axis_index("head")

    def one_pair(index, carry):
        step = index // PAIRS
        pair = lax.rem(index, PAIRS)
        head = head_group * LOCAL_HEADS + pair // 2

        def look(p, place):
            return place + jnp.where(owner[step, p] == device, p, 0)

        place = lax.fori_loop(0, SPANS, look, jnp.int32(0))
        block = (step * SPANS + place) * 2 + lax.rem(pair, 2)

        def put(slot, k, good):
            k = jnp.where(good, k, block)
            span = k // 2
            which = span // SPANS
            holder = owner[which, lax.rem(span, SPANS)]
            stored = (which * 2 + lax.rem(k, 2)) * SPANS + holder
            table[index * TILES + slot] = stored * 2 + jnp.where(good, 1, 0)

        put(0, block, block >= 0)
        picked = [vertical[head, n] for n in range(NV)]
        for n, k in enumerate(picked):
            put(1 + n, k, k < block)
        for n in range(NS):
            k = block - slash[head, n]
            good = k >= 0
            for other in picked:
                good = good & (k != other)
            put(1 + NV + n, k, good)
        return carry

    lax.fori_loop(0, STEPS * PAIRS, one_pair, 0)


def make_plan(owner, vertical, slash):
    return pl.pallas_call(
        plan_kernel,
        out_shape=jax.ShapeDtypeStruct((STEPS * PAIRS * TILES,), jnp.int32),
        in_specs=[SCALARS] * 3,
        out_specs=SCALARS,
        compiler_params=pltpu.CompilerParams(vmem_limit_bytes=MIB),
        name="plan",
    )(owner, vertical, slash)


def attend_kernel(step, table, q_hbm, *refs):
    stores = refs[: 2 * (step + 1)]
    w_hbm = refs[2 * (step + 1)]
    targets, scratch = refs[-16:-12], refs[-12:]
    q_v, kv_v, s_0, s_1, m_0, m_1, p_0, p_1, out, w_v, out_v, all_sems = scratch
    sems, w_sems, out_sems = all_sems.at[0], all_sems.at[1], all_sems.at[2:]
    core = lax.rem(lax.axis_index("head"), 2)

    copies = [pltpu.make_async_copy(q_hbm.at[step], q_v, sems.at[0])]
    for index, store in enumerate(stores):
        half = core if index % 2 == 0 else 1 - core
        start = pl.multiple_of((index // 2 * 2 + half) * SPANS, SPANS)
        copies.append(
            pltpu.make_async_copy(store, kv_v.at[pl.ds(start, SPANS)], sems.at[1 + index])
        )
    w_copies = []
    for half in range(HALVES):
        cols = pl.ds(half * WIDTH, WIDTH)
        w_copies.append(
            pltpu.make_async_copy(w_hbm.at[:, cols], w_v.at[:, cols], w_sems.at[half])
        )
    for copy in copies + w_copies:
        copy.start()
    for copy in copies:
        copy.wait()

    rows_at = lax.broadcasted_iota(jnp.int32, (BLK, BLK), 0)
    cols_at = lax.broadcasted_iota(jnp.int32, (BLK, BLK), 1)
    causal = cols_at <= rows_at
    factor = math.log2(math.e) / math.sqrt(HD)

    def columns(pair):
        return pl.ds(pl.multiple_of(pair // 2 * HD, HD), HD)

    def code_of(pair, n):
        return table[(step * PAIRS + pair) * TILES + n]

    def score(pair, inner, s_v, m_v):
        q = q_v[inner * BLK : (inner + 1) * BLK, columns(pair)]
        codes = [code_of(pair, n) for n in range(TILES)]
        keys = jnp.concatenate(
            [kv_v[lax.shift_right_logical(code, 1), 0] for code in codes], axis=0
        )
        found = lax.dot_general(
            q, keys, (((1,), (1,)), ((), ())), preferred_element_type=jnp.float32
        )
        largest = None
        for n in range(TILES):
            s = found[:, n * BLK : (n + 1) * BLK]
            s = jnp.where(causal if n == 0 else (codes[n] & 1) == 1, s, HIDDEN)
            s_v[:, n * BLK : (n + 1) * BLK] = s
            largest = s if largest is None else jnp.maximum(largest, s)
        m_v[...] = largest

    def finish(pair, inner, s_v, m_v, p_v):
        cols = columns(pair)
        chunk = 32
        totals = []
        for row in range(0, BLK, chunk):
            rows = slice(row, row + chunk)
            shift = jnp.max(m_v[rows], axis=1, keepdims=True) * factor
            total = None
            for n in range(TILES):
                at = slice(n * BLK, (n + 1) * BLK)
                w = jnp.exp2(s_v[rows, at] * factor - shift)
                p_v[rows, at] = w.astype(jnp.bfloat16)
                total = w if total is None else total + w
            totals.append(jnp.sum(total, axis=1, keepdims=True))
        values = jnp.concatenate(
            [kv_v[lax.shift_right_logical(code_of(pair, n), 1), 1] for n in range(TILES)],
            axis=0,
        )
        mixed = jnp.dot(p_v[...], values, preferred_element_type=jnp.float32)
        result = (mixed / jnp.concatenate(totals, axis=0)).astype(jnp.bfloat16)
        for group in range(BLK // 16):
            z = inner * 4 + group // 2
            start = jnp.where(core == group % 2, SPAN // 2, 0) + z * 16
            out[pl.ds(pl.multiple_of(start, 16), 16), cols] = result[group * 16 : group * 16 + 16]

    score(0, 0, s_0, m_0)

    def two_pairs(index, carry):
        pair = index * 2
        score(pair + 1, 1, s_1, m_1)
        finish(pair, 0, s_0, m_0, p_0)
        score(jnp.minimum(pair + 2, PAIRS - 2), 0, s_0, m_0)
        finish(pair + 1, 1, s_1, m_1, p_1)
        return carry

    lax.fori_loop(0, PAIRS // 2, two_pairs, 0)

    def copies_out(half, n):
        source = pl.ds(pl.multiple_of(half * WIDTH + n * TILE, TILE), TILE)
        cols = pl.ds(pl.multiple_of(n * TILE, TILE), TILE)
        return [
            pltpu.make_async_copy(
                out_v.at[pl.ds(side * (SPAN // 2), SPAN // 2), source],
                targets[half * 2 + side].at[:, cols],
                out_sems.at[half * 2 + side, n],
            )
            for side in range(2)
        ]

    tiles = WIDTH // TILE
    for half in range(HALVES):
        w_copies[half].wait()

        def one_tile(n, carry):
            cols = pl.ds(pl.multiple_of(half * WIDTH + n * TILE, TILE), TILE)
            out_v[:, cols] = jnp.dot(
                out[...], w_v[:, cols], preferred_element_type=jnp.float32
            ).astype(jnp.bfloat16)
            for copy in copies_out(half, n):
                copy.start()
            return carry

        lax.fori_loop(0, tiles, one_tile, 0)
    for half in range(HALVES):

        def end(n, carry):
            for copy in copies_out(half, n):
                copy.wait()
            return carry

        lax.fori_loop(0, tiles, end, 0)


def attend(step, table, queries, stores, weight):
    keys = TILES * BLK
    depth = LOCAL_HEADS * HD
    shape = jax.ShapeDtypeStruct((SPAN // 2, WIDTH), jnp.bfloat16)
    return pl.pallas_call(
        functools.partial(attend_kernel, step),
        out_shape=[shape] * (2 * HALVES),
        in_specs=[SCALARS] + [ANYWHERE] * (1 + len(stores)) + [IN_HBM],
        out_specs=[ANYWHERE] * (2 * HALVES),
        scratch_shapes=[
            pltpu.VMEM((SPAN, LOCAL_HEADS * HD), jnp.bfloat16),
            pltpu.VMEM(((step + 1) * 2 * SPANS, 2, BLK, HD), jnp.bfloat16),
            pltpu.VMEM((BLK, keys), jnp.float32),
            pltpu.VMEM((BLK, keys), jnp.float32),
            pltpu.VMEM((BLK, BLK), jnp.float32),
            pltpu.VMEM((BLK, BLK), jnp.float32),
            pltpu.VMEM((BLK, keys), jnp.bfloat16),
            pltpu.VMEM((BLK, keys), jnp.bfloat16),
            pltpu.VMEM((SPAN, depth), jnp.bfloat16),
            pltpu.VMEM((depth, DW), jnp.bfloat16),
            pltpu.VMEM((SPAN, DW), jnp.bfloat16),
            pltpu.SemaphoreType.DMA((6, WIDTH // TILE)),
        ],
        cost_estimate=pl.CostEstimate(
            flops=2 * SPAN * depth * DW + 4 * PAIRS * TILES * BLK * BLK * HD,
            bytes_accessed=16 * MIB,
            transcendentals=0,
        ),
        compiler_params=pltpu.CompilerParams(vmem_limit_bytes=GRANT),
    )(table, queries, *stores, weight)


def pair_sums(own, other, chips):
    def kernel(own_ref, other_ref, *outs):
        z = lax.axis_index("head") // 2
        for offset in range(chips):
            index = lax.rem(z + offset, chips)
            total = own_ref[index].astype(jnp.float32) + other_ref[index].astype(jnp.float32)
            outs[offset][...] = total.astype(jnp.bfloat16)

    shape = (chips, own.shape[0] // chips, own.shape[1])
    return pl.pallas_call(
        kernel,
        out_shape=[jax.ShapeDtypeStruct(shape[1:], own.dtype)] * chips,
        in_specs=[IN_VMEM] * 2,
        out_specs=[IN_VMEM] * chips,
        cost_estimate=pl.CostEstimate(flops=0, bytes_accessed=3 * MIB, transcendentals=0),
        compiler_params=pltpu.CompilerParams(vmem_limit_bytes=8 * MIB),
    )(own.reshape(shape), other.reshape(shape))


def local(queries, key_rows, value_rows, out_weight, span_owner, vertical_blocks, slash_offsets):
    heads = lax.axis_size("head")
    chips = heads // 2
    head_group = lax.axis_index("head")
    core = lax.rem(head_group, 2)
    kv_head = head_group * LOCAL_HEADS // (QH // KVH)
    swap = core_swap(heads)

    table = make_plan(span_owner, vertical_blocks, slash_offsets)

    weight = pltpu.with_memory_space_constraint(out_weight, pltpu.HBM)
    queries = pltpu.with_memory_space_constraint(queries, pltpu.HBM)

    def own_block(rows):
        return lax.dynamic_slice(rows, (0, core * BLK, kv_head * HD), (STEPS, BLK, HD))

    blocks = jnp.stack([own_block(key_rows), own_block(value_rows)], axis=1)
    stores = []
    streams = {}
    for step in range(STEPS):
        block = jnp.broadcast_to(blocks[step][None], (SPANS, 2, BLK, HD))
        mine = lax.all_to_all(block, "ctx", 0, 0, tiled=True)
        stores += [mine, lax.ppermute(mine, "head", swap)]
        partials = attend(step, table, queries, stores, weight)
        for half in range(HALVES):
            send, own = partials[2 * half : 2 * half + 2]
            got = lax.ppermute(send, "head", swap)
            streams[step, half] = pair_sums(own, got, chips)

    moving = {}
    far = chips // 2

    def hop(step, half, direction, number):
        longest = far if (direction == 1) == (half == 0) else far - 1
        distance = longest - number
        if distance < 1:
            return
        key = (step, half, direction)
        total = streams[step, half][(direction * distance) % chips]
        if key in moving:
            total = total.astype(jnp.float32) + moving[key].astype(jnp.float32)
        total = total.astype(jnp.bfloat16)
        moving[key] = lax.ppermute(total, "head", shift_z(heads, direction))

    for number in range(far):
        for side in (1, -1):
            for half in range(HALVES):
                for step in range(STEPS):
                    hop(step, half, side, number)

    outputs = []
    for step in range(STEPS):
        columns = []
        for half in range(HALVES):
            total = streams[step, half][0].astype(jnp.float32)
            for direction in (1, -1):
                total = total + moving[step, half, direction].astype(jnp.float32)
            columns.append(total.astype(jnp.bfloat16))
        outputs.append(jnp.concatenate(columns, axis=1)[None])
    return jnp.concatenate(outputs)


def solution(mesh):
    in_specs = (
        P(None, "ctx", "head"),
        P(None, "ctx", None),
        P(None, "ctx", None),
        P("head", None),
        P(),
        P(),
        P(),
    )
    out_specs = P(None, ("ctx", "head"), None)

    return jax.shard_map(
        local, mesh=mesh, in_specs=in_specs, out_specs=out_specs, check_vma=False
    )
```

```python
import functools
import math

import jax
import jax.numpy as jnp
from jax import lax
from jax.experimental import pallas as pl
from jax.experimental.pallas import tpu as pltpu
from jax.sharding import PartitionSpec as P


QH = 64
KVH = 4
HD = 128
BLK = 128
STEPS = 2
SPANS = 16
LOCAL_HEADS = 4
SPAN = 256
NV = 4
NS = 4
DW = 8192
TILE = 512
HALVES = 2
WIDTH = DW // HALVES
TILES = 1 + NV + NS
PAIRS = LOCAL_HEADS * 2
HIDDEN = -1e30
MIB = 1 << 20
GRANT = 24 * MIB


ANYWHERE = pl.BlockSpec(memory_space=pl.ANY)
SCALARS = pl.BlockSpec(memory_space=pltpu.SMEM)
IN_HBM = pl.BlockSpec(memory_space=pltpu.HBM)
IN_VMEM = pl.BlockSpec(memory_space=pltpu.VMEM)


def core_swap(heads):
    return [(h, h ^ 1) for h in range(heads)]


def shift_z(heads, amount):
    chips = heads // 2
    return [(h, ((h // 2 + amount) % chips) * 2 + h % 2) for h in range(heads)]


def plan_kernel(owner, vertical, slash, table):
    device = lax.axis_index("ctx")
    head_group = lax.axis_index("head")

    def one_pair(index, carry):
        step = index // PAIRS
        pair = lax.rem(index, PAIRS)
        head = head_group * LOCAL_HEADS + pair // 2

        def look(p, place):
            return place + jnp.where(owner[step, p] == device, p, 0)

        place = lax.fori_loop(0, SPANS, look, jnp.int32(0))
        block = (step * SPANS + place) * 2 + lax.rem(pair, 2)

        def put(slot, k, good):
            k = jnp.where(good, k, block)
            span = k // 2
            which = span // SPANS
            holder = owner[which, lax.rem(span, SPANS)]
            stored = (which * 2 + lax.rem(k, 2)) * SPANS + holder
            table[index * TILES + slot] = stored * 2 + jnp.where(good, 1, 0)

        put(0, block, block >= 0)
        picked = [vertical[head, n] for n in range(NV)]
        for n, k in enumerate(picked):
            put(1 + n, k, k < block)
        for n in range(NS):
            k = block - slash[head, n]
            good = k >= 0
            for other in picked:
                good = good & (k != other)
            put(1 + NV + n, k, good)
        return carry

    lax.fori_loop(0, STEPS * PAIRS, one_pair, 0)


def make_plan(owner, vertical, slash):
    return pl.pallas_call(
        plan_kernel,
        out_shape=jax.ShapeDtypeStruct((STEPS * PAIRS * TILES,), jnp.int32),
        in_specs=[SCALARS] * 3,
        out_specs=SCALARS,
        compiler_params=pltpu.CompilerParams(vmem_limit_bytes=MIB),
        name="plan",
    )(owner, vertical, slash)


def attend_kernel(step, table, q_hbm, *refs):
    stores = refs[: 2 * (step + 1)]
    w_hbm = refs[2 * (step + 1)]
    targets, scratch = refs[-14:-12], refs[-12:]
    q_v, kv_v, s_0, s_1, m_0, m_1, p_0, p_1, out, w_v, out_v, all_sems = scratch
    sems, w_sems, out_sems = all_sems.at[0], all_sems.at[1], all_sems.at[2:]
    depth = LOCAL_HEADS * HD
    w_parts = 8
    core = lax.rem(lax.axis_index("head"), 2)

    copies = [pltpu.make_async_copy(q_hbm.at[step], q_v, sems.at[0])]
    for index, store in enumerate(stores):
        half = core if index % 2 == 0 else 1 - core
        start = pl.multiple_of((index // 2 * 2 + half) * SPANS, SPANS)
        copies.append(
            pltpu.make_async_copy(store, kv_v.at[pl.ds(start, SPANS)], sems.at[1 + index])
        )
    w_copies = []
    for part in range(w_parts):
        rows = pl.ds(part * (depth // w_parts), depth // w_parts)
        w_copies.append(pltpu.make_async_copy(w_hbm.at[rows], w_v.at[rows], w_sems.at[part]))
    for copy in copies + w_copies:
        copy.start()
    for copy in copies:
        copy.wait()

    rows_at = lax.broadcasted_iota(jnp.int32, (BLK, BLK), 0)
    cols_at = lax.broadcasted_iota(jnp.int32, (BLK, BLK), 1)
    causal = cols_at <= rows_at
    factor = math.log2(math.e) / math.sqrt(HD)

    def columns(pair):
        return pl.ds(pl.multiple_of(pair // 2 * HD, HD), HD)

    def code_of(pair, n):
        return table[(step * PAIRS + pair) * TILES + n]

    def score(pair, inner, s_v, m_v):
        q = q_v[inner * BLK : (inner + 1) * BLK, columns(pair)]
        codes = [code_of(pair, n) for n in range(TILES)]
        keys = jnp.concatenate(
            [kv_v[lax.shift_right_logical(code, 1), 0] for code in codes], axis=0
        )
        found = lax.dot_general(
            q, keys, (((1,), (1,)), ((), ())), preferred_element_type=jnp.float32
        )
        largest = None
        for n in range(TILES):
            s = found[:, n * BLK : (n + 1) * BLK]
            s = jnp.where(causal if n == 0 else (codes[n] & 1) == 1, s, HIDDEN)
            s_v[:, n * BLK : (n + 1) * BLK] = s
            largest = s if largest is None else jnp.maximum(largest, s)
        m_v[...] = largest

    def finish(pair, inner, s_v, m_v, p_v):
        cols = columns(pair)
        chunk = 32
        totals = []
        for row in range(0, BLK, chunk):
            rows = slice(row, row + chunk)
            shift = jnp.max(m_v[rows], axis=1, keepdims=True) * factor
            total = None
            for n in range(TILES):
                at = slice(n * BLK, (n + 1) * BLK)
                w = jnp.exp2(s_v[rows, at] * factor - shift)
                p_v[rows, at] = w.astype(jnp.bfloat16)
                total = w if total is None else total + w
            totals.append(jnp.sum(total, axis=1, keepdims=True))
        values = jnp.concatenate(
            [kv_v[lax.shift_right_logical(code_of(pair, n), 1), 1] for n in range(TILES)],
            axis=0,
        )
        mixed = jnp.dot(p_v[...], values, preferred_element_type=jnp.float32)
        result = (mixed / jnp.concatenate(totals, axis=0)).astype(jnp.bfloat16)
        for group in range(BLK // 16):
            z = inner * 4 + group // 2
            start = jnp.where(core == group % 2, SPAN // 2, 0) + z * 16
            out[pl.ds(pl.multiple_of(start, 16), 16), cols] = result[group * 16 : group * 16 + 16]

    score(0, 0, s_0, m_0)

    def two_pairs(index, carry):
        pair = index * 2
        score(pair + 1, 1, s_1, m_1)
        finish(pair, 0, s_0, m_0, p_0)
        score(jnp.minimum(pair + 2, PAIRS - 2), 0, s_0, m_0)
        finish(pair + 1, 1, s_1, m_1, p_1)
        return carry

    lax.fori_loop(0, PAIRS // 2, two_pairs, 0)

    def copies_out(n):
        cols = pl.ds(pl.multiple_of(n * TILE, TILE), TILE)
        return [
            pltpu.make_async_copy(
                out_v.at[pl.ds(side * (SPAN // 2), SPAN // 2), cols],
                targets[side].at[:, cols],
                out_sems.at[side, n],
            )
            for side in range(2)
        ]

    tiles = DW // TILE
    for copy in w_copies:
        copy.wait()

    def one_tile(n, carry):
        cols = pl.ds(pl.multiple_of(n * TILE, TILE), TILE)
        out_v[:, cols] = jnp.dot(
            out[...], w_v[:, cols], preferred_element_type=jnp.float32
        ).astype(jnp.bfloat16)
        for copy in copies_out(n):
            copy.start()
        return carry

    lax.fori_loop(0, tiles, one_tile, 0)

    def end(n, carry):
        for copy in copies_out(n):
            copy.wait()
        return carry

    lax.fori_loop(0, tiles, end, 0)


def attend(step, table, queries, stores, weight):
    keys = TILES * BLK
    depth = LOCAL_HEADS * HD
    shape = pltpu.HBM((SPAN // 2, DW), jnp.bfloat16)
    return pl.pallas_call(
        functools.partial(attend_kernel, step),
        out_shape=[shape] * 2,
        in_specs=[SCALARS] + [ANYWHERE] * (1 + len(stores)) + [IN_HBM],
        out_specs=[IN_HBM] * 2,
        scratch_shapes=[
            pltpu.VMEM((SPAN, LOCAL_HEADS * HD), jnp.bfloat16),
            pltpu.VMEM(((step + 1) * 2 * SPANS, 2, BLK, HD), jnp.bfloat16),
            pltpu.VMEM((BLK, keys), jnp.float32),
            pltpu.VMEM((BLK, keys), jnp.float32),
            pltpu.VMEM((BLK, BLK), jnp.float32),
            pltpu.VMEM((BLK, BLK), jnp.float32),
            pltpu.VMEM((BLK, keys), jnp.bfloat16),
            pltpu.VMEM((BLK, keys), jnp.bfloat16),
            pltpu.VMEM((SPAN, depth), jnp.bfloat16),
            pltpu.VMEM((depth, DW), jnp.bfloat16),
            pltpu.VMEM((SPAN, DW), jnp.bfloat16),
            pltpu.SemaphoreType.DMA((4, DW // TILE)),
        ],
        cost_estimate=pl.CostEstimate(
            flops=2 * SPAN * depth * DW + 4 * PAIRS * TILES * BLK * BLK * HD,
            bytes_accessed=16 * MIB,
            transcendentals=0,
        ),
        compiler_params=pltpu.CompilerParams(vmem_limit_bytes=GRANT),
    )(table, queries, *stores, weight)


def waves(chips):
    far = chips // 2
    plan = []
    for number in range(far):
        for direction in (1, -1):
            distances = []
            for half in range(HALVES):
                longest = far if (direction == 1) == (half == 0) else far - 1
                if number < longest:
                    distances.append((half, direction * (longest - number)))
            plan.append((number, direction, distances))
    plan.append((far, 0, [(half, 0) for half in range(HALVES)]))
    return plan


def pair_sums(own, other, chips):
    plan = waves(chips)
    near = 2

    def kernel(own_ref, other_ref, *refs):
        outs = refs[: len(plan)]
        rest, sems = refs[len(plan) :]
        z = lax.axis_index("head") // 2
        copies = []
        row = 0
        for entry, (number, direction, distances) in enumerate(plan):
            for slot, (half, distance) in enumerate(distances):
                index = lax.rem(z + distance + chips, chips)
                cols = slice(half * WIDTH, (half + 1) * WIDTH)
                total = own_ref[index, :, cols].astype(jnp.float32)
                total = total + other_ref[index, :, cols].astype(jnp.float32)
                total = total.astype(jnp.bfloat16)
                if entry < near:
                    outs[entry][slot] = total
                else:
                    rest[row + slot] = total
            if entry >= near:
                copies.append(
                    pltpu.make_async_copy(
                        rest.at[pl.ds(row, len(distances))], outs[entry], sems.at[entry]
                    )
                )
                copies[-1].start()
                row += len(distances)
        for copy in copies:
            copy.wait()

    shape = (chips, own.shape[0] // chips, own.shape[1])
    out_shape = []
    for entry, (number, direction, distances) in enumerate(plan):
        piece = (len(distances), shape[1], WIDTH)
        if entry < near:
            out_shape.append(jax.ShapeDtypeStruct(piece, own.dtype))
        else:
            out_shape.append(pltpu.HBM(piece, own.dtype))
    later = sum(len(distances) for _, _, distances in plan[near:])
    sums = pl.pallas_call(
        kernel,
        out_shape=out_shape,
        in_specs=[IN_VMEM] * 2,
        out_specs=[IN_VMEM] * near + [IN_HBM] * (len(plan) - near),
        scratch_shapes=[
            pltpu.VMEM((later, shape[1], WIDTH), own.dtype),
            pltpu.SemaphoreType.DMA((len(plan),)),
        ],
        cost_estimate=pl.CostEstimate(flops=0, bytes_accessed=6 * MIB, transcendentals=0),
        compiler_params=pltpu.CompilerParams(vmem_limit_bytes=12 * MIB),
    )(own.reshape(shape), other.reshape(shape))
    return {(number, direction): value for (number, direction, _), value in zip(plan, sums)}


def local(queries, key_rows, value_rows, out_weight, span_owner, vertical_blocks, slash_offsets):
    heads = lax.axis_size("head")
    chips = heads // 2
    head_group = lax.axis_index("head")
    core = lax.rem(head_group, 2)
    kv_head = head_group * LOCAL_HEADS // (QH // KVH)
    swap = core_swap(heads)

    table = make_plan(span_owner, vertical_blocks, slash_offsets)

    weight = pltpu.with_memory_space_constraint(out_weight, pltpu.HBM)
    queries = pltpu.with_memory_space_constraint(queries, pltpu.HBM)

    def own_block(rows):
        return lax.dynamic_slice(rows, (0, core * BLK, kv_head * HD), (STEPS, BLK, HD))

    blocks = jnp.stack([own_block(key_rows), own_block(value_rows)], axis=1)
    stores = []
    streams = {}
    for step in range(STEPS):
        block = jnp.broadcast_to(blocks[step][None], (SPANS, 2, BLK, HD))
        mine = lax.all_to_all(block, "ctx", 0, 0, tiled=True)
        stores += [mine, lax.ppermute(mine, "head", swap)]
        send, own = attend(step, table, queries, stores, weight)
        got = lax.ppermute(send, "head", swap)
        streams[step] = pair_sums(own, got, chips)

    far = chips // 2
    moving = {}
    for number in range(far):
        for step in range(STEPS):
            for direction in (1, -1):
                total = streams[step][number, direction]
                if number > 0:
                    before = moving[step, number - 1, direction]
                    if total.shape[0] < before.shape[0]:
                        keep = 0 if direction == 1 else 1
                        moving[step, "ended", direction] = before[1 - keep]
                        before = before[keep : keep + 1]
                    total = total.astype(jnp.float32) + before.astype(jnp.float32)
                    total = total.astype(jnp.bfloat16)
                moving[step, number, direction] = lax.ppermute(
                    total, "head", shift_z(heads, direction)
                )

    outputs = []
    for step in range(STEPS):
        last = far - 1
        arrived = (
            (moving[step, last, 1][0], moving[step, "ended", -1]),
            (moving[step, "ended", 1], moving[step, last, -1][0]),
        )
        columns = []
        for half in range(HALVES):
            total = streams[step][far, 0][half].astype(jnp.float32)
            for value in arrived[half]:
                total = total + value.astype(jnp.float32)
            columns.append(total.astype(jnp.bfloat16))
        outputs.append(jnp.concatenate(columns, axis=1)[None])
    return jnp.concatenate(outputs)


def solution(mesh):
    in_specs = (
        P(None, "ctx", "head"),
        P(None, "ctx", None),
        P(None, "ctx", None),
        P("head", None),
        P(),
        P(),
        P(),
    )
    out_specs = P(None, ("ctx", "head"), None)

    return jax.shard_map(
        local, mesh=mesh, in_specs=in_specs, out_specs=out_specs, check_vma=False
    )
```

```python
import functools
import math

import jax
import jax.numpy as jnp
from jax import lax
from jax.experimental import pallas as pl
from jax.experimental.pallas import tpu as pltpu
from jax.sharding import PartitionSpec as P


QH = 64
KVH = 4
HD = 128
BLK = 128
STEPS = 2
SPANS = 16
LOCAL_HEADS = 4
SPAN = 256
NV = 4
NS = 4
DW = 8192
TILE = 512
HALVES = 2
WIDTH = DW // HALVES
TILES = 1 + NV + NS
PAIRS = LOCAL_HEADS * 2
HIDDEN = -1e30
MIB = 1 << 20
GRANT = 24 * MIB


ANYWHERE = pl.BlockSpec(memory_space=pl.ANY)
SCALARS = pl.BlockSpec(memory_space=pltpu.SMEM)
IN_HBM = pl.BlockSpec(memory_space=pltpu.HBM)
IN_VMEM = pl.BlockSpec(memory_space=pltpu.VMEM)


def core_swap(heads):
    return [(h, h ^ 1) for h in range(heads)]


def shift_z(heads, amount):
    chips = heads // 2
    return [(h, ((h // 2 + amount) % chips) * 2 + h % 2) for h in range(heads)]


def plan_kernel(owner, vertical, slash, table):
    device = lax.axis_index("ctx")
    head_group = lax.axis_index("head")

    def one_pair(index, carry):
        step = index // PAIRS
        pair = lax.rem(index, PAIRS)
        head = head_group * LOCAL_HEADS + pair // 2

        def look(p, place):
            return place + jnp.where(owner[step, p] == device, p, 0)

        place = lax.fori_loop(0, SPANS, look, jnp.int32(0))
        block = (step * SPANS + place) * 2 + lax.rem(pair, 2)

        def put(slot, k, good):
            k = jnp.where(good, k, block)
            span = k // 2
            which = span // SPANS
            holder = owner[which, lax.rem(span, SPANS)]
            stored = (which * 2 + lax.rem(k, 2)) * SPANS + holder
            table[index * TILES + slot] = stored * 2 + jnp.where(good, 1, 0)

        put(0, block, block >= 0)
        picked = [vertical[head, n] for n in range(NV)]
        for n, k in enumerate(picked):
            put(1 + n, k, k < block)
        for n in range(NS):
            k = block - slash[head, n]
            good = k >= 0
            for other in picked:
                good = good & (k != other)
            put(1 + NV + n, k, good)
        return carry

    lax.fori_loop(0, STEPS * PAIRS, one_pair, 0)


def make_plan(owner, vertical, slash):
    return pl.pallas_call(
        plan_kernel,
        out_shape=jax.ShapeDtypeStruct((STEPS * PAIRS * TILES,), jnp.int32),
        in_specs=[SCALARS] * 3,
        out_specs=SCALARS,
        compiler_params=pltpu.CompilerParams(vmem_limit_bytes=MIB),
        name="plan",
    )(owner, vertical, slash)


def attend_kernel(step, joined, table, q_hbm, *refs):
    stores = refs[: 2 * (step + 1)]
    if joined:
        w_hbm = refs[2 * (step + 1)]
        targets, scratch = refs[-14:-12], refs[-12:]
        q_v, kv_v, s_0, s_1, m_0, m_1, p_0, p_1, out, w_v, out_v, all_sems = scratch
    else:
        out, q_v, kv_v, s_0, s_1, m_0, m_1, p_0, p_1, all_sems = refs[-10:]
    sems = all_sems.at[0]
    depth = LOCAL_HEADS * HD
    w_parts = 8 if joined else 0
    core = lax.rem(lax.axis_index("head"), 2)

    copies = [pltpu.make_async_copy(q_hbm.at[step], q_v, sems.at[0])]
    for index, store in enumerate(stores):
        half = core if index % 2 == 0 else 1 - core
        start = pl.multiple_of((index // 2 * 2 + half) * SPANS, SPANS)
        copies.append(
            pltpu.make_async_copy(store, kv_v.at[pl.ds(start, SPANS)], sems.at[1 + index])
        )
    w_copies = []
    for part in range(w_parts):
        rows = pl.ds(part * (depth // w_parts), depth // w_parts)
        w_copies.append(pltpu.make_async_copy(w_hbm.at[rows], w_v.at[rows], all_sems.at[1, part]))
    for copy in copies + w_copies:
        copy.start()
    for copy in copies:
        copy.wait()

    rows_at = lax.broadcasted_iota(jnp.int32, (BLK, BLK), 0)
    cols_at = lax.broadcasted_iota(jnp.int32, (BLK, BLK), 1)
    causal = cols_at <= rows_at
    factor = math.log2(math.e) / math.sqrt(HD)

    def columns(pair):
        return pl.ds(pl.multiple_of(pair // 2 * HD, HD), HD)

    def code_of(pair, n):
        return table[(step * PAIRS + pair) * TILES + n]

    def score(pair, inner, s_v, m_v):
        q = q_v[inner * BLK : (inner + 1) * BLK, columns(pair)]
        codes = [code_of(pair, n) for n in range(TILES)]
        keys = jnp.concatenate(
            [kv_v[lax.shift_right_logical(code, 1), 0] for code in codes], axis=0
        )
        found = lax.dot_general(
            q, keys, (((1,), (1,)), ((), ())), preferred_element_type=jnp.float32
        )
        largest = None
        for n in range(TILES):
            s = found[:, n * BLK : (n + 1) * BLK]
            s = jnp.where(causal if n == 0 else (codes[n] & 1) == 1, s, HIDDEN)
            s_v[:, n * BLK : (n + 1) * BLK] = s
            largest = s if largest is None else jnp.maximum(largest, s)
        m_v[...] = largest

    def finish(pair, inner, s_v, m_v, p_v):
        cols = columns(pair)
        chunk = 32
        totals = []
        for row in range(0, BLK, chunk):
            rows = slice(row, row + chunk)
            shift = jnp.max(m_v[rows], axis=1, keepdims=True) * factor
            total = None
            for n in range(TILES):
                at = slice(n * BLK, (n + 1) * BLK)
                w = jnp.exp2(s_v[rows, at] * factor - shift)
                p_v[rows, at] = w.astype(jnp.bfloat16)
                total = w if total is None else total + w
            totals.append(jnp.sum(total, axis=1, keepdims=True))
        values = jnp.concatenate(
            [kv_v[lax.shift_right_logical(code_of(pair, n), 1), 1] for n in range(TILES)],
            axis=0,
        )
        mixed = jnp.dot(p_v[...], values, preferred_element_type=jnp.float32)
        result = (mixed / jnp.concatenate(totals, axis=0)).astype(jnp.bfloat16)
        for group in range(BLK // 16):
            z = inner * 4 + group // 2
            start = jnp.where(core == group % 2, SPAN // 2, 0) + z * 16
            out[pl.ds(pl.multiple_of(start, 16), 16), cols] = result[group * 16 : group * 16 + 16]

    score(0, 0, s_0, m_0)

    def two_pairs(index, carry):
        pair = index * 2
        score(pair + 1, 1, s_1, m_1)
        finish(pair, 0, s_0, m_0, p_0)
        score(jnp.minimum(pair + 2, PAIRS - 2), 0, s_0, m_0)
        finish(pair + 1, 1, s_1, m_1, p_1)
        return carry

    lax.fori_loop(0, PAIRS // 2, two_pairs, 0)

    if not joined:
        return
    for copy in w_copies:
        copy.wait()
    project_tiles(out, w_v, out_v, targets, all_sems.at[2:], lambda n: None)


def project_tiles(left, w_v, out_v, targets, out_sems, ready):
    def copies_out(n):
        cols = pl.ds(pl.multiple_of(n * TILE, TILE), TILE)
        return [
            pltpu.make_async_copy(
                out_v.at[pl.ds(side * (SPAN // 2), SPAN // 2), cols],
                targets[side].at[:, cols],
                out_sems.at[side, n],
            )
            for side in range(2)
        ]

    tiles = DW // TILE

    def one_tile(n, carry):
        cols = pl.ds(pl.multiple_of(n * TILE, TILE), TILE)
        ready(n)
        out_v[:, cols] = jnp.dot(
            left[...], w_v[:, cols], preferred_element_type=jnp.float32
        ).astype(jnp.bfloat16)
        for copy in copies_out(n):
            copy.start()
        return carry

    lax.fori_loop(0, tiles, one_tile, 0)

    def end(n, carry):
        for copy in copies_out(n):
            copy.wait()
        return carry

    lax.fori_loop(0, tiles, end, 0)


def project_kernel(attended, w_hbm, send, own, w_v, out_v, sems):
    def copy_in(n):
        cols = pl.ds(pl.multiple_of(n * TILE, TILE), TILE)
        return pltpu.make_async_copy(w_hbm.at[:, cols], w_v.at[:, cols], sems.at[0, n])

    for n in range(DW // TILE):
        copy_in(n).start()
    project_tiles(attended, w_v, out_v, (send, own), sems.at[1:], lambda n: copy_in(n).wait())


def project(attended, weight):
    depth = LOCAL_HEADS * HD
    shape = pltpu.HBM((SPAN // 2, DW), jnp.bfloat16)
    return pl.pallas_call(
        project_kernel,
        out_shape=[shape] * 2,
        in_specs=[IN_VMEM, IN_HBM],
        out_specs=[IN_HBM] * 2,
        scratch_shapes=[
            pltpu.VMEM((depth, DW), jnp.bfloat16),
            pltpu.VMEM((SPAN, DW), jnp.bfloat16),
            pltpu.SemaphoreType.DMA((3, DW // TILE)),
        ],
        cost_estimate=pl.CostEstimate(
            flops=2 * SPAN * depth * DW, bytes_accessed=12 * MIB, transcendentals=0
        ),
        compiler_params=pltpu.CompilerParams(vmem_limit_bytes=GRANT),
    )(attended, weight)


def attend(step, table, queries, stores, weight):
    keys = TILES * BLK
    depth = LOCAL_HEADS * HD
    joined = weight is not None
    scratch = [
        pltpu.VMEM((SPAN, depth), jnp.bfloat16),
        pltpu.VMEM(((step + 1) * 2 * SPANS, 2, BLK, HD), jnp.bfloat16),
        pltpu.VMEM((BLK, keys), jnp.float32),
        pltpu.VMEM((BLK, keys), jnp.float32),
        pltpu.VMEM((BLK, BLK), jnp.float32),
        pltpu.VMEM((BLK, BLK), jnp.float32),
        pltpu.VMEM((BLK, keys), jnp.bfloat16),
        pltpu.VMEM((BLK, keys), jnp.bfloat16),
    ]
    flops = 4 * PAIRS * TILES * BLK * BLK * HD
    if joined:
        scratch += [
            pltpu.VMEM((SPAN, depth), jnp.bfloat16),
            pltpu.VMEM((depth, DW), jnp.bfloat16),
            pltpu.VMEM((SPAN, DW), jnp.bfloat16),
        ]
        out_shape = [pltpu.HBM((SPAN // 2, DW), jnp.bfloat16)] * 2
        out_specs = [IN_HBM] * 2
        flops += 2 * SPAN * depth * DW
    else:
        out_shape = jax.ShapeDtypeStruct((SPAN, depth), jnp.bfloat16)
        out_specs = IN_VMEM
    scratch.append(pltpu.SemaphoreType.DMA((4, DW // TILE)))
    extra = [weight] if joined else []
    return pl.pallas_call(
        functools.partial(attend_kernel, step, joined),
        out_shape=out_shape,
        in_specs=[SCALARS] + [ANYWHERE] * (1 + len(stores)) + [IN_HBM] * len(extra),
        out_specs=out_specs,
        scratch_shapes=scratch,
        cost_estimate=pl.CostEstimate(
            flops=flops, bytes_accessed=16 * MIB, transcendentals=0
        ),
        compiler_params=pltpu.CompilerParams(vmem_limit_bytes=GRANT),
    )(table, queries, *stores, *extra)


def waves(chips):
    far = chips // 2
    plan = []
    for number in range(far):
        for direction in (1, -1):
            distances = []
            for half in range(HALVES):
                longest = far if (direction == 1) == (half == 0) else far - 1
                if number < longest:
                    distances.append((half, direction * (longest - number)))
            plan.append((number, direction, distances))
    plan.append((far, 0, [(half, 0) for half in range(HALVES)]))
    return plan


def pair_sums(own, other, chips):
    plan = waves(chips)
    near = 2

    def kernel(own_hbm, other_ref, *refs):
        outs = refs[: len(plan)]
        rest, own_ref, sems = refs[len(plan) :]
        z = lax.axis_index("head") // 2
        copies = []
        row = 0
        moves = [
            [
                pltpu.make_async_copy(
                    own_hbm.at[
                        lax.rem(z + distance + chips, chips), :, pl.ds(half * WIDTH, WIDTH)
                    ],
                    own_ref.at[entry, slot],
                    sems.at[1, HALVES * entry + slot],
                )
                for slot, (half, distance) in enumerate(distances)
            ]
            for entry, (number, direction, distances) in enumerate(plan)
        ]
        for entry_moves in moves:
            for move in entry_moves:
                move.start()
        for entry, (number, direction, distances) in enumerate(plan):
            for slot, (half, distance) in enumerate(distances):
                index = lax.rem(z + distance + chips, chips)
                cols = slice(half * WIDTH, (half + 1) * WIDTH)
                moves[entry][slot].wait()
                total = own_ref[entry, slot].astype(jnp.float32)
                total = total + other_ref[index, :, cols].astype(jnp.float32)
                total = total.astype(jnp.bfloat16)
                if entry < near:
                    outs[entry][slot] = total
                else:
                    rest[row + slot] = total
            if entry >= near:
                copies.append(
                    pltpu.make_async_copy(
                        rest.at[pl.ds(row, len(distances))], outs[entry], sems.at[0, entry]
                    )
                )
                copies[-1].start()
                row += len(distances)
        for copy in copies:
            copy.wait()

    shape = (chips, own.shape[0] // chips, own.shape[1])
    out_shape = []
    for entry, (number, direction, distances) in enumerate(plan):
        piece = (len(distances), shape[1], WIDTH)
        if entry < near:
            out_shape.append(jax.ShapeDtypeStruct(piece, own.dtype))
        else:
            out_shape.append(pltpu.HBM(piece, own.dtype))
    later = sum(len(distances) for _, _, distances in plan[near:])
    sums = pl.pallas_call(
        kernel,
        out_shape=out_shape,
        in_specs=[IN_HBM, IN_VMEM],
        out_specs=[IN_VMEM] * near + [IN_HBM] * (len(plan) - near),
        scratch_shapes=[
            pltpu.VMEM((later, shape[1], WIDTH), own.dtype),
            pltpu.VMEM((len(plan), HALVES, shape[1], WIDTH), own.dtype),
            pltpu.SemaphoreType.DMA((2, HALVES * len(plan))),
        ],
        cost_estimate=pl.CostEstimate(flops=0, bytes_accessed=6 * MIB, transcendentals=0),
        compiler_params=pltpu.CompilerParams(vmem_limit_bytes=12 * MIB),
    )(pltpu.with_memory_space_constraint(own.reshape(shape), pltpu.HBM), other.reshape(shape))
    return {(number, direction): value for (number, direction, _), value in zip(plan, sums)}


def local(queries, key_rows, value_rows, out_weight, span_owner, vertical_blocks, slash_offsets):
    heads = lax.axis_size("head")
    chips = heads // 2
    head_group = lax.axis_index("head")
    core = lax.rem(head_group, 2)
    kv_head = head_group * LOCAL_HEADS // (QH // KVH)
    swap = core_swap(heads)

    table = make_plan(span_owner, vertical_blocks, slash_offsets)

    weight = pltpu.with_memory_space_constraint(out_weight, pltpu.HBM)
    queries = pltpu.with_memory_space_constraint(queries, pltpu.HBM)

    def own_block(rows):
        return lax.dynamic_slice(rows, (0, core * BLK, kv_head * HD), (STEPS, BLK, HD))

    blocks = jnp.stack([own_block(key_rows), own_block(value_rows)], axis=1)
    stores = []
    streams = {}
    for step in range(STEPS):
        block = jnp.broadcast_to(blocks[step][None], (SPANS, 2, BLK, HD))
        mine = lax.all_to_all(block, "ctx", 0, 0, tiled=True)
        stores += [mine, lax.ppermute(mine, "head", swap)]
        if step == 0:
            send, own = attend(step, table, queries, stores, weight)
        else:
            send, own = project(attend(step, table, queries, stores, None), weight)
        got = lax.ppermute(send, "head", swap)
        streams[step] = pair_sums(own, got, chips)

    far = chips // 2
    moving = {}
    for number in range(far):
        for step in range(STEPS):
            for direction in (1, -1):
                total = streams[step][number, direction]
                if number > 0:
                    before = moving[step, number - 1, direction]
                    if total.shape[0] < before.shape[0]:
                        keep = 0 if direction == 1 else 1
                        moving[step, "ended", direction] = before[1 - keep]
                        before = before[keep : keep + 1]
                    total = total.astype(jnp.float32) + before.astype(jnp.float32)
                    total = total.astype(jnp.bfloat16)
                moving[step, number, direction] = lax.ppermute(
                    total, "head", shift_z(heads, direction)
                )

    outputs = []
    for step in range(STEPS):
        last = far - 1
        arrived = (
            (moving[step, last, 1][0], moving[step, "ended", -1]),
            (moving[step, "ended", 1], moving[step, last, -1][0]),
        )
        columns = []
        for half in range(HALVES):
            total = streams[step][far, 0][half].astype(jnp.float32)
            for value in arrived[half]:
                total = total + value.astype(jnp.float32)
            columns.append(total.astype(jnp.bfloat16))
        outputs.append(jnp.concatenate(columns, axis=1)[None])
    return jnp.concatenate(outputs)


def solution(mesh):
    in_specs = (
        P(None, "ctx", "head"),
        P(None, "ctx", None),
        P(None, "ctx", None),
        P("head", None),
        P(),
        P(),
        P(),
    )
    out_specs = P(None, ("ctx", "head"), None)

    return jax.shard_map(local, mesh=mesh, in_specs=in_specs, out_specs=out_specs, check_vma=False)
```

```python
import functools
import math

import jax
import jax.numpy as jnp
from jax import lax
from jax.experimental import pallas as pl
from jax.experimental.pallas import tpu as pltpu
from jax.sharding import PartitionSpec as P


QH = 64
KVH = 4
HD = 128
BLK = 128
STEPS = 2
SPANS = 16
LOCAL_HEADS = 4
SPAN = 256
NV = 4
NS = 4
DW = 8192
TILE = 512
HALVES = 2
WIDTH = DW // HALVES
TILES = 1 + NV + NS
PAIRS = LOCAL_HEADS * 2
HIDDEN = -1e30
MIB = 1 << 20
GRANT = 24 * MIB


ANYWHERE = pl.BlockSpec(memory_space=pl.ANY)
SCALARS = pl.BlockSpec(memory_space=pltpu.SMEM)
IN_HBM = pl.BlockSpec(memory_space=pltpu.HBM)
IN_VMEM = pl.BlockSpec(memory_space=pltpu.VMEM)


def core_swap(heads):
    return [(h, h ^ 1) for h in range(heads)]


def shift_z(heads, amount):
    chips = heads // 2
    return [(h, ((h // 2 + amount) % chips) * 2 + h % 2) for h in range(heads)]


def plan_kernel(owner, vertical, slash, table):
    device = lax.axis_index("ctx")
    head_group = lax.axis_index("head")

    def one_pair(index, carry):
        step = index // PAIRS
        pair = lax.rem(index, PAIRS)
        head = head_group * LOCAL_HEADS + pair // 2

        def look(p, place):
            return place + jnp.where(owner[step, p] == device, p, 0)

        place = lax.fori_loop(0, SPANS, look, jnp.int32(0))
        block = (step * SPANS + place) * 2 + lax.rem(pair, 2)

        def put(slot, k, good):
            k = jnp.where(good, k, block)
            span = k // 2
            which = span // SPANS
            holder = owner[which, lax.rem(span, SPANS)]
            stored = (which * 2 + lax.rem(k, 2)) * SPANS + holder
            table[index * TILES + slot] = stored * 2 + jnp.where(good, 1, 0)

        put(0, block, block >= 0)
        picked = [vertical[head, n] for n in range(NV)]
        for n, k in enumerate(picked):
            put(1 + n, k, k < block)
        for n in range(NS):
            k = block - slash[head, n]
            good = k >= 0
            for other in picked:
                good = good & (k != other)
            put(1 + NV + n, k, good)
        return carry

    lax.fori_loop(0, STEPS * PAIRS, one_pair, 0)


def make_plan(owner, vertical, slash):
    return pl.pallas_call(
        plan_kernel,
        out_shape=jax.ShapeDtypeStruct((STEPS * PAIRS * TILES,), jnp.int32),
        in_specs=[SCALARS] * 3,
        out_specs=SCALARS,
        compiler_params=pltpu.CompilerParams(vmem_limit_bytes=MIB),
        name="plan",
    )(owner, vertical, slash)


def attend_kernel(step, joined, table, q_hbm, *refs):
    stores = refs[: 2 * (step + 1)]
    if joined:
        w_hbm = refs[2 * (step + 1)]
        targets, scratch = refs[-14:-12], refs[-12:]
        q_v, kv_v, s_0, s_1, m_0, m_1, p_0, p_1, out, w_v, out_v, all_sems = scratch
    else:
        out, q_v, kv_v, s_0, s_1, m_0, m_1, p_0, p_1, all_sems = refs[-10:]
    sems = all_sems.at[0]
    depth = LOCAL_HEADS * HD
    w_parts = 8 if joined else 0
    core = lax.rem(lax.axis_index("head"), 2)

    copies = [pltpu.make_async_copy(q_hbm.at[step], q_v, sems.at[0])]
    for index, store in enumerate(stores):
        half = core if index % 2 == 0 else 1 - core
        start = pl.multiple_of((index // 2 * 2 + half) * SPANS, SPANS)
        copies.append(
            pltpu.make_async_copy(store, kv_v.at[pl.ds(start, SPANS)], sems.at[1 + index])
        )
    w_copies = []
    for part in range(w_parts):
        rows = pl.ds(part * (depth // w_parts), depth // w_parts)
        w_copies.append(pltpu.make_async_copy(w_hbm.at[rows], w_v.at[rows], all_sems.at[1, part]))
    for copy in copies + w_copies:
        copy.start()
    for copy in copies:
        copy.wait()

    rows_at = lax.broadcasted_iota(jnp.int32, (BLK, BLK), 0)
    cols_at = lax.broadcasted_iota(jnp.int32, (BLK, BLK), 1)
    causal = cols_at <= rows_at
    factor = math.log2(math.e) / math.sqrt(HD)

    def columns(pair):
        return pl.ds(pl.multiple_of(pair // 2 * HD, HD), HD)

    def code_of(pair, n):
        return table[(step * PAIRS + pair) * TILES + n]

    def score(pair, inner, s_v, m_v):
        q = q_v[inner * BLK : (inner + 1) * BLK, columns(pair)]
        codes = [code_of(pair, n) for n in range(TILES)]
        keys = jnp.concatenate(
            [kv_v[lax.shift_right_logical(code, 1), 0] for code in codes], axis=0
        )
        found = lax.dot_general(
            q, keys, (((1,), (1,)), ((), ())), preferred_element_type=jnp.float32
        )
        largest = None
        for n in range(TILES):
            s = found[:, n * BLK : (n + 1) * BLK]
            s = jnp.where(causal if n == 0 else (codes[n] & 1) == 1, s, HIDDEN)
            s_v[:, n * BLK : (n + 1) * BLK] = s
            largest = s if largest is None else jnp.maximum(largest, s)
        m_v[...] = largest

    def finish(pair, inner, s_v, m_v, p_v):
        cols = columns(pair)
        chunk = 32
        totals = []
        for row in range(0, BLK, chunk):
            rows = slice(row, row + chunk)
            shift = jnp.max(m_v[rows], axis=1, keepdims=True) * factor
            total = None
            for n in range(TILES):
                at = slice(n * BLK, (n + 1) * BLK)
                w = jnp.exp2(s_v[rows, at] * factor - shift)
                p_v[rows, at] = w.astype(jnp.bfloat16)
                total = w if total is None else total + w
            totals.append(jnp.sum(total, axis=1, keepdims=True))
        values = jnp.concatenate(
            [kv_v[lax.shift_right_logical(code_of(pair, n), 1), 1] for n in range(TILES)],
            axis=0,
        )
        mixed = jnp.dot(p_v[...], values, preferred_element_type=jnp.float32)
        result = (mixed / jnp.concatenate(totals, axis=0)).astype(jnp.bfloat16)
        for group in range(BLK // 16):
            z = inner * 4 + group // 2
            start = jnp.where(core == group % 2, SPAN // 2, 0) + z * 16
            out[pl.ds(pl.multiple_of(start, 16), 16), cols] = result[group * 16 : group * 16 + 16]

    score(0, 0, s_0, m_0)

    def two_pairs(index, carry):
        pair = index * 2
        score(pair + 1, 1, s_1, m_1)
        finish(pair, 0, s_0, m_0, p_0)
        score(jnp.minimum(pair + 2, PAIRS - 2), 0, s_0, m_0)
        finish(pair + 1, 1, s_1, m_1, p_1)
        return carry

    lax.fori_loop(0, PAIRS // 2, two_pairs, 0)

    if not joined:
        return
    for copy in w_copies:
        copy.wait()
    project_tiles(out, w_v, out_v, targets, all_sems.at[2:], lambda n: None)


def project_tiles(left, w_v, out_v, targets, out_sems, ready):
    def copies_out(n):
        cols = pl.ds(pl.multiple_of(n * TILE, TILE), TILE)
        return [
            pltpu.make_async_copy(
                out_v.at[pl.ds(side * (SPAN // 2), SPAN // 2), cols],
                targets[side].at[:, cols],
                out_sems.at[side, n],
            )
            for side in range(2)
        ]

    tiles = DW // TILE

    def one_tile(n, carry):
        cols = pl.ds(pl.multiple_of(n * TILE, TILE), TILE)
        ready(n)
        out_v[:, cols] = jnp.dot(
            left[...], w_v[:, cols], preferred_element_type=jnp.float32
        ).astype(jnp.bfloat16)
        for copy in copies_out(n):
            copy.start()
        return carry

    lax.fori_loop(0, tiles, one_tile, 0)

    def end(n, carry):
        for copy in copies_out(n):
            copy.wait()
        return carry

    lax.fori_loop(0, tiles, end, 0)


def project_kernel(attended, w_hbm, send, own, w_v, out_v, sems):
    def copy_in(n):
        cols = pl.ds(pl.multiple_of(n * TILE, TILE), TILE)
        return pltpu.make_async_copy(w_hbm.at[:, cols], w_v.at[:, cols], sems.at[0, n])

    for n in range(DW // TILE):
        copy_in(n).start()
    project_tiles(attended, w_v, out_v, (send, own), sems.at[1:], lambda n: copy_in(n).wait())


def project(attended, weight):
    depth = LOCAL_HEADS * HD
    shape = pltpu.HBM((SPAN // 2, DW), jnp.bfloat16)
    return pl.pallas_call(
        project_kernel,
        out_shape=[shape] * 2,
        in_specs=[IN_VMEM, IN_HBM],
        out_specs=[IN_HBM] * 2,
        scratch_shapes=[
            pltpu.VMEM((depth, DW), jnp.bfloat16),
            pltpu.VMEM((SPAN, DW), jnp.bfloat16),
            pltpu.SemaphoreType.DMA((3, DW // TILE)),
        ],
        cost_estimate=pl.CostEstimate(
            flops=2 * SPAN * depth * DW, bytes_accessed=12 * MIB, transcendentals=0
        ),
        compiler_params=pltpu.CompilerParams(vmem_limit_bytes=GRANT),
    )(attended, weight)


def attend(step, table, queries, stores, weight):
    keys = TILES * BLK
    depth = LOCAL_HEADS * HD
    joined = weight is not None
    scratch = [
        pltpu.VMEM((SPAN, depth), jnp.bfloat16),
        pltpu.VMEM(((step + 1) * 2 * SPANS, 2, BLK, HD), jnp.bfloat16),
        pltpu.VMEM((BLK, keys), jnp.float32),
        pltpu.VMEM((BLK, keys), jnp.float32),
        pltpu.VMEM((BLK, BLK), jnp.float32),
        pltpu.VMEM((BLK, BLK), jnp.float32),
        pltpu.VMEM((BLK, keys), jnp.bfloat16),
        pltpu.VMEM((BLK, keys), jnp.bfloat16),
    ]
    flops = 4 * PAIRS * TILES * BLK * BLK * HD
    if joined:
        scratch += [
            pltpu.VMEM((SPAN, depth), jnp.bfloat16),
            pltpu.VMEM((depth, DW), jnp.bfloat16),
            pltpu.VMEM((SPAN, DW), jnp.bfloat16),
        ]
        out_shape = [pltpu.HBM((SPAN // 2, DW), jnp.bfloat16)] * 2
        out_specs = [IN_HBM] * 2
        flops += 2 * SPAN * depth * DW
    else:
        out_shape = jax.ShapeDtypeStruct((SPAN, depth), jnp.bfloat16)
        out_specs = IN_VMEM
    scratch.append(pltpu.SemaphoreType.DMA((4, DW // TILE)))
    extra = [weight] if joined else []
    return pl.pallas_call(
        functools.partial(attend_kernel, step, joined),
        out_shape=out_shape,
        in_specs=[SCALARS] + [ANYWHERE] * (1 + len(stores)) + [IN_HBM] * len(extra),
        out_specs=out_specs,
        scratch_shapes=scratch,
        cost_estimate=pl.CostEstimate(
            flops=flops, bytes_accessed=16 * MIB, transcendentals=0
        ),
        compiler_params=pltpu.CompilerParams(vmem_limit_bytes=GRANT),
    )(table, queries, *stores, *extra)


def waves(chips, merged):
    far = chips // 2
    plan = []
    for number in range(far + 1):
        for direction in (1, -1) if number < far else (0,):
            distances = []
            for half in range(HALVES):
                longest = far if (direction == 1) == (half == 0) else far - 1
                if direction == 0:
                    distances.append((half, 0))
                elif number < longest:
                    distances.append((half, direction * (longest - number)))
            if merged:
                plan.append((number, direction, distances))
            else:
                plan += [(number, direction, [entry]) for entry in distances]
    return plan


def pair_sums(step, own, other, chips):
    merged = step == 0
    plan = waves(chips, merged)
    near = 2 if merged else 2 * HALVES

    def kernel(own_hbm, other_ref, *refs):
        outs = refs[: len(plan)]
        rest, own_ref, sems = refs[len(plan) :]
        z = lax.axis_index("head") // 2
        copies = []
        row = 0
        moves = [
            [
                pltpu.make_async_copy(
                    own_hbm.at[
                        lax.rem(z + distance + chips, chips), :, pl.ds(half * WIDTH, WIDTH)
                    ],
                    own_ref.at[entry, slot],
                    sems.at[1, HALVES * entry + slot],
                )
                for slot, (half, distance) in enumerate(distances)
            ]
            for entry, (number, direction, distances) in enumerate(plan)
        ]
        for entry_moves in moves:
            for move in entry_moves:
                move.start()
        for entry, (number, direction, distances) in enumerate(plan):
            for slot, (half, distance) in enumerate(distances):
                index = lax.rem(z + distance + chips, chips)
                cols = slice(half * WIDTH, (half + 1) * WIDTH)
                moves[entry][slot].wait()
                total = own_ref[entry, slot].astype(jnp.float32)
                total = total + other_ref[index, :, cols].astype(jnp.float32)
                total = total.astype(jnp.bfloat16)
                if entry < near:
                    outs[entry][slot] = total
                else:
                    rest[row + slot] = total
            if entry >= near:
                copies.append(
                    pltpu.make_async_copy(
                        rest.at[pl.ds(row, len(distances))], outs[entry], sems.at[0, entry]
                    )
                )
                copies[-1].start()
                row += len(distances)
        for copy in copies:
            copy.wait()

    shape = (chips, own.shape[0] // chips, own.shape[1])
    out_shape = []
    for entry, (number, direction, distances) in enumerate(plan):
        piece = (len(distances), shape[1], WIDTH)
        if entry < near:
            out_shape.append(jax.ShapeDtypeStruct(piece, own.dtype))
        else:
            out_shape.append(pltpu.HBM(piece, own.dtype))
    later = sum(len(distances) for _, _, distances in plan[near:])
    sums = pl.pallas_call(
        kernel,
        out_shape=out_shape,
        in_specs=[IN_HBM, IN_VMEM],
        out_specs=[IN_VMEM] * near + [IN_HBM] * (len(plan) - near),
        scratch_shapes=[
            pltpu.VMEM((later, shape[1], WIDTH), own.dtype),
            pltpu.VMEM((len(plan), HALVES if merged else 1, shape[1], WIDTH), own.dtype),
            pltpu.SemaphoreType.DMA((2, HALVES * len(plan))),
        ],
        cost_estimate=pl.CostEstimate(flops=0, bytes_accessed=6 * MIB, transcendentals=0),
        compiler_params=pltpu.CompilerParams(vmem_limit_bytes=12 * MIB),
    )(pltpu.with_memory_space_constraint(own.reshape(shape), pltpu.HBM), other.reshape(shape))
    if merged:
        return {(number, direction): value for (number, direction, _), value in zip(plan, sums)}
    return {
        (number, direction, distances[0][0]): value
        for (number, direction, distances), value in zip(plan, sums)
    }


def local(queries, key_rows, value_rows, out_weight, span_owner, vertical_blocks, slash_offsets):
    heads = lax.axis_size("head")
    chips = heads // 2
    head_group = lax.axis_index("head")
    core = lax.rem(head_group, 2)
    kv_head = head_group * LOCAL_HEADS // (QH // KVH)
    swap = core_swap(heads)

    table = make_plan(span_owner, vertical_blocks, slash_offsets)

    weight = pltpu.with_memory_space_constraint(out_weight, pltpu.HBM)
    queries = pltpu.with_memory_space_constraint(queries, pltpu.HBM)

    def own_block(rows):
        return lax.dynamic_slice(rows, (0, core * BLK, kv_head * HD), (STEPS, BLK, HD))

    blocks = jnp.stack([own_block(key_rows), own_block(value_rows)], axis=1)
    stores = []
    streams = {}
    for step in range(STEPS):
        block = jnp.broadcast_to(blocks[step][None], (SPANS, 2, BLK, HD))
        mine = lax.all_to_all(block, "ctx", 0, 0, tiled=True)
        stores += [mine, lax.ppermute(mine, "head", swap)]
        if step == 0:
            send, own = attend(step, table, queries, stores, weight)
        else:
            send, own = project(attend(step, table, queries, stores, None), weight)
        got = lax.ppermute(send, "head", swap)
        streams[step] = pair_sums(step, own, got, chips)

    far = chips // 2
    moving = {}
    for number in range(far):
        for direction in (1, -1):
            total = streams[0][number, direction]
            if number > 0:
                before = moving[number - 1, direction]
                if total.shape[0] < before.shape[0]:
                    keep = 0 if direction == 1 else 1
                    moving["ended", direction] = before[1 - keep]
                    before = before[keep : keep + 1]
                total = total.astype(jnp.float32) + before.astype(jnp.float32)
                total = total.astype(jnp.bfloat16)
            moving[number, direction] = lax.ppermute(
                total, "head", shift_z(heads, direction)
            )
    last = {}
    for number in range(far):
        for direction in (1, -1):
            for half in range(HALVES):
                if (number, direction, half) not in streams[1]:
                    continue
                total = streams[1][number, direction, half]
                if number > 0:
                    total = total.astype(jnp.float32) + last[direction, half].astype(jnp.float32)
                    total = total.astype(jnp.bfloat16)
                last[direction, half] = lax.ppermute(
                    total, "head", shift_z(heads, direction)
                )

    arrived = (
        (moving[far - 1, 1][0], moving["ended", -1]),
        (moving["ended", 1], moving[far - 1, -1][0]),
    )
    outputs = []
    for step in range(STEPS):
        columns = []
        for half in range(HALVES):
            if step == 0:
                total = streams[0][far, 0][half].astype(jnp.float32)
                values = arrived[half]
            else:
                total = streams[1][far, 0, half][0].astype(jnp.float32)
                values = (last[1, half][0], last[-1, half][0])
            for value in values:
                total = total + value.astype(jnp.float32)
            columns.append(total.astype(jnp.bfloat16))
        outputs.append(jnp.concatenate(columns, axis=1)[None])
    return jnp.concatenate(outputs)


def solution(mesh):
    in_specs = (
        P(None, "ctx", "head"),
        P(None, "ctx", None),
        P(None, "ctx", None),
        P("head", None),
        P(),
        P(),
        P(),
    )
    out_specs = P(None, ("ctx", "head"), None)

    return jax.shard_map(local, mesh=mesh, in_specs=in_specs, out_specs=out_specs, check_vma=False)
```
